256 devices in a mesh: dp: 32 (over y, x, core), mp: 8 (over z).
Axes of the slice: x: 4, y: 4, z: 8, core: 2. Of those that a mesh axis runs over, the one named last changes fastest.
Arguments:
- image_latents: bfloat16 [64, 48, 3072], P('dp', None, 'mp'), may hold values from -6 to 6
- text_states: bfloat16 [448, 16, 3072], P('dp', None, 'mp'), may hold values from -6 to 6
- modulation: bfloat16 [448, 3, 3072], P('dp', None, 'mp'), may hold values from -2 to 2
- w_qkv: bfloat16 [3072, 3, 2048], P(None, None, 'mp'), may hold values from -0.109375 to 0.109375
- w_out: bfloat16 [2048, 3072], P('mp'), may hold values from -0.125 to 0.125
- q_gain: float32 [128], replicated, may hold values from 1.2 to 3
- k_gain: float32 [128], replicated, may hold values from 1.2 to 3
- branch_count: int32 [64], P('dp'), may hold values from 1 to 7, as said below
- branch_sign: int32 [448], P('dp'), may hold values from 0 to 1
- guide_weight: int32 [448], P('dp'), may hold values from 1 to 8
Outputs:
- prediction: bfloat16 [64, 48, 3072], P('dp', None, 'mp')
The draws below stay inside these ranges and needn't reach their ends.
Inputs may be any that keep to these rules, and one draw needn't show every extreme that they name: `branch_count`: image i and image i + 32 have counts summing to 8, so the counts of all images sum to 256.
All inputs are finite; a program needn't handle non-finite values.
Results may differ from the reference program's by a relative error of at most 0.015.
Values may be sent and summed in bfloat16 or wider, within the bound.
No kernel may reach another device: no remote copies, remote signals or barrier semaphores. Data moves between devices by JAX's collectives and lax.ppermute only.
A program may use at most 64 MiB of HBM per device.

```python
import math
import jax
import jax.numpy as jnp
from jax import lax

D = 3072
HEADS = 16
HD = 128
IMG_TOK = 48
TXT_TOK = 16
MAXB = 7
IMG_DEV = 2
IMAGES = 64
L = 64
N_MP = 8


def draw_branch_count(key, part):
    count_key = jax.random.fold_in(key, 11)
    half_count = IMAGES // 2
    first_counts = jax.random.randint(count_key, (half_count,), 1, MAXB + 1)
    first_counts = jnp.where(jnp.arange(half_count) < IMG_DEV, MAXB, first_counts)
    return jnp.concatenate([first_counts, MAXB + 1 - first_counts]).astype(jnp.int32)


def draw_modulation(key, part):
    slot_rows = IMAGES * MAXB
    base_key = jax.random.fold_in(key, 23)
    shift_key = jax.random.fold_in(base_key, 1)
    scale_key = jax.random.fold_in(base_key, 2)
    gate_key = jax.random.fold_in(base_key, 3)
    sign_key = jax.random.fold_in(base_key, 4)
    shift_rows = 0.25 * jax.random.truncated_normal(shift_key, -3.0, 3.0, (slot_rows, 1, D), jnp.float32)
    scale_rows = jax.random.uniform(scale_key, (slot_rows, 1, D), jnp.float32, 0.0, 1.5)
    magnitude = jax.random.uniform(gate_key, (slot_rows, 1, D), jnp.float32, 0.75, 2.0)
    sign_rows = jnp.where(jax.random.bernoulli(sign_key, 0.5, (slot_rows, 1, D)), 1.0, -1.0).astype(jnp.float32)
    gate_rows = sign_rows * magnitude
    return jnp.concatenate([shift_rows, scale_rows, gate_rows], axis=1).astype(jnp.bfloat16)


def with_ends(array, stream_key, least, high):
    longest = array.shape.index(max(array.shape))
    spots = []
    for shift in (0, 1):
        where = [jax.random.randint(jax.random.fold_in(stream_key, axis), (), 0, length) for axis, length in enumerate(array.shape)]
        where[longest] = (where[longest] + shift) % array.shape[longest]
        spots.append(tuple(where))
    return array.at[spots[0]].set(least).at[spots[1]].set(high)


def steps_of(stream_key, dims, cuts, low, high):
    loudness, own = 1.0, jax.random.fold_in(stream_key, 6)
    for axis_at, parts in cuts:
        draws = jnp.exp(jax.random.uniform(jax.random.fold_in(own, axis_at), (parts,), jnp.float32, low / len(cuts), high / len(cuts)))
        loudness = loudness * jnp.repeat(draws, dims[axis_at] // parts).reshape([-1 if axis == axis_at else 1 for axis in range(len(dims))])
    return loudness


def normal_values(rng, dims, width, reach, split=(), kind=jnp.bfloat16):
    entries = jax.random.normal(rng, dims, jnp.float32) * width
    if len(split) > 0:
        entries = steps_of(rng, dims, split, -0.22, 0.18) * entries
    return jnp.clip(entries, min=-reach, max=reach).astype(kind)


def setup_inputs(seed: int = 0) -> dict:
    splits = jax.random.split(jax.random.key(seed), 11)
    return {
        "image_latents": normal_values(splits[0], (IMAGES, IMG_TOK, D), 1.0, 6.0, ((0, 32), (2, 8))),
        "text_states": normal_values(splits[1], (IMAGES * MAXB, TXT_TOK, D), 1.0, 6.0, ((0, 32), (2, 8))),
        "modulation": draw_modulation(jax.random.fold_in(splits[10], 71), 0),
        "w_qkv": normal_values(splits[3], (D, 3, HEADS * HD), D ** -0.5, 0.109375, ((2, 8),)),
        "w_out": normal_values(splits[4], (HEADS * HD, D), (HEADS * HD) ** -0.5, 0.125, ((0, 8),)),
        "q_gain": jnp.clip(jnp.exp(jax.random.uniform(splits[5], (HD,), jnp.float32, math.log(1.2), math.log(3.0))), 1.2, 3.0),
        "k_gain": jnp.clip(jnp.exp(jax.random.uniform(splits[6], (HD,), jnp.float32, math.log(1.2), math.log(3.0))), 1.2, 3.0),
        "branch_count": draw_branch_count(jax.random.fold_in(splits[10], 71), 0),
        "branch_sign": with_ends(jax.random.randint(splits[8], (IMAGES * MAXB,), 0, 2), jax.random.fold_in(splits[8], 1), 0, 1).astype(jnp.int32),
        "guide_weight": with_ends(jax.random.randint(splits[9], (IMAGES * MAXB,), 1, 9), jax.random.fold_in(splits[9], 1), 1, 8).astype(jnp.int32),
    }


epsilon = 1e-06

def rms_norm(values, gain):
    return values * lax.rsqrt(lax.optimization_barrier(jnp.mean(values * values, axis=-1, keepdims=True)) + epsilon) * gain

def block_row(sequence, modulation_rows, w_qkv, w_out, q_gain, k_gain):
    states = sequence.astype(jnp.float32)
    row_mean = lax.optimization_barrier(jnp.mean(states, axis=-1, keepdims=True))
    centered = states - row_mean
    spread = lax.optimization_barrier(jnp.mean(centered * centered, axis=-1, keepdims=True))
    shift_rows = modulation_rows[0].astype(jnp.float32)
    scale_rows = modulation_rows[1].astype(jnp.float32)
    gate_rows = modulation_rows[2].astype(jnp.float32)
    normed = (centered * lax.rsqrt(spread + epsilon) * (1.0 + scale_rows) + shift_rows).astype(jnp.bfloat16)
    projected = jnp.dot(normed, w_qkv.reshape(D, 3 * HEADS * HD), preferred_element_type=jnp.float32)
    projected = projected.reshape(L, 3, HEADS, HD)
    queries = rms_norm(projected[:, 0], q_gain).astype(jnp.bfloat16)
    key_rows = rms_norm(projected[:, 1], k_gain).astype(jnp.bfloat16)
    value_rows = projected[:, 2].astype(jnp.bfloat16)
    scores = jnp.einsum('qhd,khd->hqk', queries.astype(jnp.float32), key_rows.astype(jnp.float32)) * HD ** (-0.5)
    attention_weights = jax.nn.softmax(scores, axis=-1).astype(jnp.bfloat16)
    attended = jnp.einsum('hqk,khd->qhd', attention_weights.astype(jnp.float32), value_rows.astype(jnp.float32)).astype(jnp.bfloat16)
    group_heads = HEADS // N_MP
    image_part = attended[TXT_TOK:].reshape(IMG_TOK, N_MP, group_heads * HD)
    partials = jnp.einsum('tgc,gcd->gtd', image_part.astype(jnp.float32), w_out.reshape(N_MP, group_heads * HD, D).astype(jnp.float32))
    partials = lax.optimization_barrier(partials.astype(jnp.bfloat16)).astype(jnp.float32)
    out_rows = lax.optimization_barrier(jnp.sum(partials, axis=0))
    return (states[TXT_TOK:] + gate_rows * out_rows).astype(jnp.bfloat16)

def reference(image_latents, text_states, modulation, w_qkv, w_out, q_gain, k_gain, branch_count, branch_sign, guide_weight):
    is_live = jnp.arange(MAXB, dtype=jnp.int32)[None, :] < branch_count[:, None]
    weights_live = jnp.where(is_live, guide_weight.reshape(IMAGES, MAXB), 0).astype(jnp.float32)
    weight_total = lax.optimization_barrier(jnp.sum(weights_live, axis=1))
    branch_slots = jnp.nonzero(is_live.reshape(-1), size=4 * IMAGES)[0].astype(jnp.int32)
    branch_image = (branch_slots // MAXB).astype(jnp.int32)
    signs = (2 * branch_sign[branch_slots] - 1).astype(jnp.float32)
    coefficient = signs * guide_weight[branch_slots].astype(jnp.float32) / weight_total[branch_image]

    def branch_output(slot_index):
        image_index = (slot_index // MAXB).astype(jnp.int32)
        sequence = jnp.concatenate([text_states[slot_index], image_latents[image_index]], axis=0)
        return block_row(sequence, modulation[slot_index], w_qkv, w_out, q_gain, k_gain)
    outputs = lax.map(branch_output, branch_slots)
    weighted = coefficient[:, None, None] * outputs.astype(jnp.float32)
    prediction = jax.ops.segment_sum(weighted, branch_image, num_segments=IMAGES)
    return prediction.astype(jnp.bfloat16)
```

```python
import jax
import jax.numpy as jnp
from jax import lax
from jax.experimental import pallas as pl
from jax.experimental.pallas import tpu as pltpu
from jax.sharding import PartitionSpec as P

epsilon = 1e-06
ROUND = 16


def up(rows):
    return -(-rows // ROUND) * ROUND


class Sizes:
    def __init__(self, images, image_len, slots, text_len, width, peers, head_dim, local_cols):
        self.images, self.image_len, self.slots, self.text_len = images, image_len, slots, text_len
        self.width, self.peers, self.head_dim, self.cols = width, peers, head_dim, local_cols
        self.per_image = slots // images
        self.seq = image_len + text_len
        self.image_rows = images * image_len
        self.token_rows = self.image_rows + slots * text_len
        self.mod_rows = up(slots + 1)
        self.shift_at = self.token_rows
        self.scale_at = self.shift_at + self.mod_rows
        self.gate_at = self.scale_at + self.mod_rows
        self.payload = self.gate_at + self.mod_rows
        self.cut = up(self.payload // 2)
        self.seq_rows = slots * self.seq
        self.work_rows = self.seq_rows + 2 * self.mod_rows


def accumulate(sz, place_ref, shards, w_ref, mod_ref, y_ref, s1_ref, s2_ref, c_ref, first):
    width, lanes = sz.width, 128
    s1 = None
    for at, (offset, payload) in enumerate(shards):
        tokens = payload[0 : sz.token_rows, :].astype(jnp.float32)
        if first and at == 0:
            center = jnp.broadcast_to(
                jnp.sum(tokens, axis=1, keepdims=True) * (1.0 / width), (sz.token_rows, lanes)
            )
            c_ref[...] = center
        elif at == 0:
            center = c_ref[...]
        tokens = tokens - jnp.concatenate([center] * (width // lanes), axis=1)
        squares = tokens * tokens
        for part in range(width // lanes):
            piece = tokens[:, part * lanes : (part + 1) * lanes]
            piece2 = squares[:, part * lanes : (part + 1) * lanes]
            if s1 is None:
                s1, s2 = piece, piece2
            else:
                s1, s2 = s1 + piece, s2 + piece2
        cols = slice(at * width, (at + 1) * width)
        scale = payload[sz.scale_at : sz.scale_at + sz.mod_rows, :].astype(jnp.float32)
        row = lax.broadcasted_iota(jnp.int32, scale.shape, 0)
        scale_one = jnp.where(row == sz.slots, 1.0, scale)
        for s in range(sz.slots):
            image = s // sz.per_image
            factor = 1.0 + scale[s : s + 1, :]
            picture = tokens[image * sz.image_len : (image + 1) * sz.image_len, :]
            text_at = sz.image_rows + s * sz.text_len
            text = tokens[text_at : text_at + sz.text_len, :]
            base = s * sz.seq
            mod_ref[base : base + sz.image_len, cols] = (picture * factor).astype(jnp.bfloat16)
            mod_ref[base + sz.image_len : base + sz.seq, cols] = (text * factor).astype(jnp.bfloat16)
        mod_ref[sz.seq_rows : sz.seq_rows + sz.mod_rows, cols] = scale_one.astype(jnp.bfloat16)
        mod_ref[sz.seq_rows + sz.mod_rows : sz.work_rows, cols] = payload[
            sz.shift_at : sz.shift_at + sz.mod_rows, :
        ]
    if first:
        s1_ref[...] = s1
        s2_ref[...] = s2
    else:
        s1_ref[...] += s1
        s2_ref[...] += s2
    for third in range(3):
        weights = jnp.concatenate(
            [
                w_ref[third, pl.ds(pl.multiple_of(place_ref[offset] * width, 128), width), :]
                for offset, _ in shards
            ],
            axis=0,
        )
        part = jnp.dot(
            mod_ref[:, 0 : len(shards) * width], weights, preferred_element_type=jnp.float32
        )
        if first:
            y_ref[third] = part
        else:
            y_ref[third] += part


def rms_norm(values, gain):
    return values * lax.rsqrt(jnp.mean(values * values, axis=-1, keepdims=True) + epsilon) * gain


def finish(sz, place_ref, payloads, w_out_ref, coef_ref, q_gain_ref, k_gain_ref, y_ref, s1_ref, s2_ref, att_ref, out_refs):
    full = float(sz.width * sz.peers)
    mean = jnp.sum(s1_ref[...], axis=1, keepdims=True) * (1.0 / full)
    second = jnp.sum(s2_ref[...], axis=1, keepdims=True) * (1.0 / full)
    rstd = lax.rsqrt(jnp.maximum(second - mean * mean, 0.0) + epsilon)
    lift = -mean * rstd
    q_gain, k_gain = q_gain_ref[...], k_gain_ref[...]
    head_dim = sz.head_dim
    ones_at = sz.seq_rows + sz.slots
    for s in range(sz.slots):
        image = s // sz.per_image
        text_at = sz.image_rows + s * sz.text_len
        scale_at, shift_at, base = sz.seq_rows + s, sz.seq_rows + sz.mod_rows + s, s * sz.seq
        i0, i1 = image * sz.image_len, (image + 1) * sz.image_len
        r = jnp.concatenate([rstd[i0:i1], rstd[text_at : text_at + sz.text_len]], axis=0)
        m = jnp.concatenate([lift[i0:i1], lift[text_at : text_at + sz.text_len]], axis=0)

        def projected(third, head, rows):
            cs = slice(head * head_dim, (head + 1) * head_dim)
            u = y_ref[third, scale_at : scale_at + 1, cs] + y_ref[third, ones_at : ones_at + 1, cs]
            v = y_ref[third, shift_at : shift_at + 1, cs]
            return y_ref[third, base : base + rows, cs] * r[:rows] + (m[:rows] * u + v)

        for head in range(sz.cols // head_dim):
            q = rms_norm(projected(0, head, sz.image_len), q_gain).astype(jnp.bfloat16)
            k = rms_norm(projected(1, head, sz.seq), k_gain).astype(jnp.bfloat16)
            v = projected(2, head, sz.seq).astype(jnp.bfloat16)
            scores = lax.dot_general(
                q, k, (((1,), (1,)), ((), ())), preferred_element_type=jnp.float32
            ) * head_dim ** (-0.5)
            e = jnp.exp(scores - jnp.max(scores, axis=1, keepdims=True))
            probs = (e / jnp.sum(e, axis=1, keepdims=True)).astype(jnp.bfloat16)
            att = jnp.dot(probs, v, preferred_element_type=jnp.float32).astype(jnp.bfloat16)
            att_ref[
                s * sz.image_len : (s + 1) * sz.image_len, head * head_dim : (head + 1) * head_dim
            ] = att
    for offset in range(sz.peers):
        cols = pl.ds(pl.multiple_of(place_ref[offset] * sz.width, 128), sz.width)
        rows = jnp.dot(att_ref[...], w_out_ref[:, cols], preferred_element_type=jnp.float32)
        gate_from = payloads[offset]
        gates = gate_from[0][gate_from[1] : gate_from[1] + sz.mod_rows, :].astype(jnp.float32)
        for image in range(sz.images):
            total = None
            for s in range(image * sz.per_image, (image + 1) * sz.per_image):
                term = rows[s * sz.image_len : (s + 1) * sz.image_len, :] * (
                    gates[s : s + 1, :] * coef_ref[s]
                )
                total = term if total is None else total + term
            out_refs[offset][image * sz.image_len : (image + 1) * sz.image_len, :] = total.astype(
                jnp.bfloat16
            )


VM = pl.BlockSpec(memory_space=pltpu.VMEM)
SM = pl.BlockSpec(memory_space=pltpu.SMEM)
PARAMS = pltpu.CompilerParams(vmem_limit_bytes=40 * 1024 * 1024)


def state_shapes(sz):
    f32 = jnp.float32
    return [
        jax.ShapeDtypeStruct((3, sz.work_rows, sz.cols), f32),
        jax.ShapeDtypeStruct((sz.token_rows, 128), f32),
        jax.ShapeDtypeStruct((sz.token_rows, 128), f32),
        jax.ShapeDtypeStruct((sz.token_rows, 128), f32),
    ]


def add_shards(sz, place, offsets, payloads, w, state, name):
    first = state is None
    count = len(offsets)

    def body(place_ref, *refs):
        payload_refs, refs = refs[:count], refs[count:]
        w_ref, refs = refs[0], refs[1:]
        if not first:
            refs = refs[4:]
        y_ref, s1_ref, s2_ref, c_ref, mod_ref = refs
        accumulate(
            sz,
            place_ref,
            list(zip(offsets, payload_refs)),
            w_ref,
            mod_ref,
            y_ref,
            s1_ref,
            s2_ref,
            c_ref,
            first,
        )

    operands = [place, *payloads, w] + ([] if first else list(state))
    aliases = {} if first else {2 + count + i: i for i in range(4)}
    return pl.pallas_call(
        body,
        out_shape=state_shapes(sz),
        in_specs=[SM] + [VM] * (len(operands) - 1),
        out_specs=[VM] * 4,
        scratch_shapes=[pltpu.VMEM((sz.work_rows, count * sz.width), jnp.bfloat16)],
        input_output_aliases=aliases,
        compiler_params=PARAMS,
        name=name,
    )(*operands)


def last_shard(sz, place, ring, top, bottom, w, w_out, coef, q_gain, k_gain, state):
    far = sz.peers // 2
    near = [o for o in range(sz.peers) if o != far]

    def body(place_ref, coef_ref, *refs):
        near_refs, refs = refs[: len(near)], refs[len(near) :]
        top_ref, bottom_ref, w_ref, w_out_ref, q_gain_ref, k_gain_ref = refs[:6]
        y_in, s1_in, s2_in, c_in = refs[6:10]
        out_refs = refs[10 : 10 + sz.peers]
        mod_ref, att_ref, whole_ref, y_ref, s1_ref, s2_ref = refs[10 + sz.peers :]
        whole_ref[0 : sz.cut, :] = top_ref[...]
        whole_ref[sz.cut :, :] = bottom_ref[...]
        s1_ref[...] = s1_in[...]
        s2_ref[...] = s2_in[...]
        y_ref[...] = y_in[...]
        accumulate(
            sz, place_ref, [(far, whole_ref)], w_ref, mod_ref, y_ref, s1_ref, s2_ref, c_in, False
        )
        payloads = {o: (ref, sz.gate_at) for o, ref in zip(near, near_refs)}
        payloads[far] = (whole_ref, sz.gate_at)
        finish(
            sz,
            place_ref,
            payloads,
            w_out_ref,
            coef_ref,
            q_gain_ref,
            k_gain_ref,
            y_ref,
            s1_ref,
            s2_ref,
            att_ref,
            out_refs,
        )

    operands = [place, coef] + [ring[o] for o in near]
    operands += [top, bottom, w, w_out, q_gain, k_gain, *state]
    return pl.pallas_call(
        body,
        out_shape=[jax.ShapeDtypeStruct((sz.image_rows, sz.width), jnp.bfloat16)] * sz.peers,
        in_specs=[SM, SM] + [VM] * (len(operands) - 2),
        out_specs=[VM] * sz.peers,
        scratch_shapes=[
            pltpu.VMEM((sz.work_rows, sz.width), jnp.bfloat16),
            pltpu.VMEM((sz.slots * sz.image_len, sz.cols), jnp.bfloat16),
            pltpu.VMEM((sz.payload, sz.width), jnp.bfloat16),
            pltpu.VMEM((3, sz.work_rows, sz.cols), jnp.float32),
            pltpu.VMEM((sz.token_rows, 128), jnp.float32),
            pltpu.VMEM((sz.token_rows, 128), jnp.float32),
        ],
        compiler_params=PARAMS,
        name="attend_project",
    )(*operands)


def on_device(
    image_latents,
    text_states,
    modulation,
    w_qkv,
    w_out,
    q_gain,
    k_gain,
    branch_count,
    branch_sign,
    guide_weight,
):
    images, image_len, width = image_latents.shape
    slots, text_len, _ = text_states.shape
    peers = lax.axis_size("mp")
    sz = Sizes(images, image_len, slots, text_len, width, peers, q_gain.shape[0], w_out.shape[0])

    modulation_rows = jnp.pad(
        jnp.transpose(modulation, (1, 0, 2)), ((0, 0), (0, sz.mod_rows - slots), (0, 0))
    )
    payload = jnp.concatenate(
        [
            image_latents.reshape(sz.image_rows, width),
            text_states.reshape(slots * text_len, width),
            modulation_rows.reshape(3 * sz.mod_rows, width),
        ],
        axis=0,
    )
    w = jnp.transpose(w_qkv, (1, 0, 2))
    place = (lax.axis_index("mp") + jnp.arange(peers, dtype=jnp.int32)) % peers

    is_live = (jnp.arange(sz.per_image, dtype=jnp.int32)[None, :] < branch_count[:, None]).reshape(-1)
    weights_live = jnp.where(is_live, guide_weight, 0).astype(jnp.float32)
    weight_total = jnp.sum(weights_live.reshape(images, sz.per_image), axis=1)
    coef = (2 * branch_sign - 1).astype(jnp.float32) * weights_live / jnp.repeat(weight_total, sz.per_image)
    coef_total = jnp.sum(coef.reshape(images, sz.per_image), axis=1)

    def shifted(x, by):
        return lax.ppermute(x, "mp", [(i, (i + by) % peers) for i in range(peers)])

    far = peers // 2
    ring = {0: payload}
    below = above = payload
    state = None
    for step in range(1, far):
        below, above = shifted(below, 1), shifted(above, -1)
        ring[peers - step], ring[step] = below, above
        offsets = [peers - step, step] if step > 1 else [0, peers - step, step]
        state = add_shards(
            sz, place, offsets, [ring[o] for o in offsets], w, state, f"project_{step}"
        )
    top, bottom = shifted(below[: sz.cut], 1), shifted(above[sz.cut :], -1)
    parts = last_shard(
        sz,
        place,
        ring,
        top,
        bottom,
        w,
        w_out,
        coef,
        q_gain.reshape(1, -1),
        k_gain.reshape(1, -1),
        state,
    )
    total = parts[0].astype(jnp.float32)
    order = [far] + [o for d in range(far - 1, 0, -1) for o in (d, peers - d)]
    for offset in order:
        total = total + shifted(parts[offset], offset).astype(jnp.float32)
    total = total.reshape(images, image_len, width)
    return (image_latents.astype(jnp.float32) * coef_total[:, None, None] + total).astype(jnp.bfloat16)


def solution(mesh):
    placed = (
        P("dp", None, "mp"),
        P("dp", None, "mp"),
        P("dp", None, "mp"),
        P(None, None, "mp"),
        P("mp", None),
        P(),
        P(),
        P("dp"),
        P("dp"),
        P("dp"),
    )
    return jax.shard_map(
        on_device, mesh=mesh, in_specs=placed, out_specs=P("dp", None, "mp"), check_vma=False
    )
```

```python
import jax
import jax.numpy as jnp
from jax import lax
from jax.experimental import pallas as pl
from jax.experimental.pallas import tpu as pltpu
from jax.sharding import PartitionSpec as P

epsilon = 1e-06
ROUND = 16


def up(rows):
    return -(-rows // ROUND) * ROUND


class Sizes:
    def __init__(self, images, image_len, slots, text_len, width, peers, head_dim, local_cols):
        self.images, self.image_len, self.slots, self.text_len = images, image_len, slots, text_len
        self.width, self.peers, self.head_dim, self.cols = width, peers, head_dim, local_cols
        self.per_image = slots // images
        self.seq = image_len + text_len
        self.image_rows = images * image_len
        self.token_rows = self.image_rows + slots * text_len
        self.mod_rows = up(slots + 1)
        self.shift_at = self.token_rows
        self.scale_at = self.shift_at + self.mod_rows
        self.gate_at = self.scale_at + self.mod_rows
        self.payload = self.gate_at + self.mod_rows
        self.cut = up(self.payload // 2)
        self.seq_rows = slots * self.seq
        self.work_rows = self.seq_rows + 2 * self.mod_rows


def accumulate(sz, place_ref, shards, w_ref, mod_ref, y_refs, s1_refs, s2_refs, c_ref):
    width, lanes = sz.width, 128
    (y_in, y_ref), (s1_in, s1_ref), (s2_in, s2_ref) = y_refs, s1_refs, s2_refs
    first = y_in is None
    s1 = None
    for at, (offset, payload) in enumerate(shards):
        tokens = payload[0 : sz.token_rows, :].astype(jnp.float32)
        if first and at == 0:
            center = jnp.broadcast_to(
                jnp.sum(tokens, axis=1, keepdims=True) * (1.0 / width), (sz.token_rows, lanes)
            )
            c_ref[...] = center
        elif at == 0:
            center = c_ref[...]
        tokens = tokens - jnp.concatenate([center] * (width // lanes), axis=1)
        squares = tokens * tokens
        for part in range(width // lanes):
            piece = tokens[:, part * lanes : (part + 1) * lanes]
            piece2 = squares[:, part * lanes : (part + 1) * lanes]
            if s1 is None:
                s1, s2 = piece, piece2
            else:
                s1, s2 = s1 + piece, s2 + piece2
        cols = slice(at * width, (at + 1) * width)
        scale = payload[sz.scale_at : sz.scale_at + sz.mod_rows, :].astype(jnp.float32)
        row = lax.broadcasted_iota(jnp.int32, scale.shape, 0)
        scale_one = jnp.where(row == sz.slots, 1.0, scale)
        for s in range(sz.slots):
            image = s // sz.per_image
            factor = 1.0 + scale[s : s + 1, :]
            picture = tokens[image * sz.image_len : (image + 1) * sz.image_len, :]
            text_at = sz.image_rows + s * sz.text_len
            text = tokens[text_at : text_at + sz.text_len, :]
            base = s * sz.seq
            mod_ref[base : base + sz.image_len, cols] = (picture * factor).astype(jnp.bfloat16)
            mod_ref[base + sz.image_len : base + sz.seq, cols] = (text * factor).astype(jnp.bfloat16)
        mod_ref[sz.seq_rows : sz.seq_rows + sz.mod_rows, cols] = scale_one.astype(jnp.bfloat16)
        mod_ref[sz.seq_rows + sz.mod_rows : sz.work_rows, cols] = payload[
            sz.shift_at : sz.shift_at + sz.mod_rows, :
        ]
    if first:
        s1_ref[...] = s1
        s2_ref[...] = s2
    else:
        s1_ref[...] = s1_in[...] + s1
        s2_ref[...] = s2_in[...] + s2
    for third in range(3):
        weights = jnp.concatenate(
            [
                w_ref[third, pl.ds(pl.multiple_of(place_ref[offset] * width, 128), width), :]
                for offset, _ in shards
            ],
            axis=0,
        )
        part = jnp.dot(
            mod_ref[:, 0 : len(shards) * width], weights, preferred_element_type=jnp.float32
        )
        if first:
            y_ref[third] = part
        else:
            y_ref[third] = y_in[third] + part


def rms_norm(values, gain):
    return values * lax.rsqrt(jnp.mean(values * values, axis=-1, keepdims=True) + epsilon) * gain


def attend(sz, q_gain_ref, k_gain_ref, y_ref, s1_ref, s2_ref, rb_ref, mb_ref, q_ref, k_ref, v_ref, sums_ref, scores_ref, att_ref):
    full = float(sz.width * sz.peers)
    dim, heads, seq, pic = sz.head_dim, sz.cols // sz.head_dim, sz.seq, sz.image_len
    mean = jnp.sum(s1_ref[...], axis=1, keepdims=True) * (1.0 / full)
    second = jnp.sum(s2_ref[...], axis=1, keepdims=True) * (1.0 / full)
    rstd = lax.rsqrt(jnp.maximum(second - mean * mean, 0.0) + epsilon)
    rb_ref[...] = jnp.broadcast_to(rstd, (sz.token_rows, 128))
    mb_ref[...] = jnp.broadcast_to(-mean * rstd, (sz.token_rows, 128))
    q_gain, k_gain = q_gain_ref[...], k_gain_ref[...]
    ones_at = sz.seq_rows + sz.slots
    zeros = jnp.zeros((seq, dim), jnp.bfloat16)
    ones = jnp.ones((seq, dim), jnp.bfloat16)
    for h in range(heads):
        for g in range(heads):
            sums_ref[h * seq : (h + 1) * seq, g * dim : (g + 1) * dim] = ones if g == h else zeros
    for s in range(sz.slots):
        image = s // sz.per_image
        text_at = sz.image_rows + s * sz.text_len
        scale_at, shift_at, base = sz.seq_rows + s, sz.seq_rows + sz.mod_rows + s, s * seq
        spans = [
            (0, pic, image * pic),
            (pic, seq, text_at),
        ]
        for h in range(heads):
            cs = slice(h * dim, (h + 1) * dim)
            for third in range(3):
                u = y_ref[third, scale_at : scale_at + 1, cs] + y_ref[third, ones_at : ones_at + 1, cs]
                v = y_ref[third, shift_at : shift_at + 1, cs]
                for lo, hi, at in spans[: 1 if third == 0 else 2]:
                    rows = slice(at, at + hi - lo)
                    value = y_ref[third, base + lo : base + hi, cs] * rb_ref[rows, :]
                    value = value + (mb_ref[rows, :] * u + v)
                    if third == 0:
                        q_ref[s, :, cs] = rms_norm(value, q_gain).astype(jnp.bfloat16)
                    else:
                        if third == 1:
                            value = rms_norm(value, k_gain)
                        out = k_ref if third == 1 else v_ref
                        out[s, h * seq + lo : h * seq + hi, cs] = value.astype(jnp.bfloat16)
            for g in range(heads):
                if g != h:
                    k_ref[s, h * seq : (h + 1) * seq, g * dim : (g + 1) * dim] = zeros
                    v_ref[s, h * seq : (h + 1) * seq, g * dim : (g + 1) * dim] = zeros
    for s in range(sz.slots):
        scores_ref[s] = lax.dot_general(
            q_ref[s], k_ref[s], (((1,), (1,)), ((), ())), preferred_element_type=jnp.float32
        ) * dim ** (-0.5)
    lane = lax.broadcasted_iota(jnp.int32, (pic, heads * seq), 1)
    sums_rhs = sums_ref[...]
    for s in range(sz.slots):
        scores = scores_ref[s]
        top = None
        for h in range(heads):
            mine = (lane >= h * seq) & (lane < (h + 1) * seq)
            peak = jnp.max(jnp.where(mine, scores, -jnp.inf), axis=1, keepdims=True)
            top = jnp.broadcast_to(peak, scores.shape) if top is None else jnp.where(mine, peak, top)
        e = jnp.exp(scores - top).astype(jnp.bfloat16)
        total = jnp.dot(e, sums_rhs, preferred_element_type=jnp.float32)
        mixed = jnp.dot(e, v_ref[s], preferred_element_type=jnp.float32)
        att_ref[s * pic : (s + 1) * pic, :] = (mixed / total).astype(jnp.bfloat16)


def project_out(sz, place_ref, offsets, gate_rows, w_out_ref, coef_ref, att_ref, out_refs):
    for offset, gates, out_ref in zip(offsets, gate_rows, out_refs):
        cols = pl.ds(pl.multiple_of(place_ref[offset] * sz.width, 128), sz.width)
        rows = jnp.dot(att_ref[...], w_out_ref[:, cols], preferred_element_type=jnp.float32)
        for image in range(sz.images):
            total = None
            for s in range(image * sz.per_image, (image + 1) * sz.per_image):
                term = rows[s * sz.image_len : (s + 1) * sz.image_len, :] * (
                    gates[s : s + 1, :] * coef_ref[s]
                )
                total = term if total is None else total + term
            out_ref[image * sz.image_len : (image + 1) * sz.image_len, :] = total.astype(jnp.bfloat16)


VM = pl.BlockSpec(memory_space=pltpu.VMEM)
SM = pl.BlockSpec(memory_space=pltpu.SMEM)
PARAMS = pltpu.CompilerParams(vmem_limit_bytes=40 * 1024 * 1024)


def state_shapes(sz):
    f32 = jnp.float32
    return [
        jax.ShapeDtypeStruct((3, sz.work_rows, sz.cols), f32),
        jax.ShapeDtypeStruct((sz.token_rows, 128), f32),
        jax.ShapeDtypeStruct((sz.token_rows, 128), f32),
        jax.ShapeDtypeStruct((sz.token_rows, 128), f32),
    ]


def add_shards(sz, place, offsets, payloads, w, state, name):
    first = state is None
    count = len(offsets)

    def body(place_ref, *refs):
        payload_refs, refs = refs[:count], refs[count:]
        w_ref, refs = refs[0], refs[1:]
        y_in, s1_in, s2_in, c_in = (None, None, None, refs[3]) if first else refs[:4]
        if not first:
            refs = refs[4:]
        y_ref, s1_ref, s2_ref, c_ref, mod_ref = refs
        accumulate(
            sz,
            place_ref,
            list(zip(offsets, payload_refs)),
            w_ref,
            mod_ref,
            (y_in, y_ref),
            (s1_in, s1_ref),
            (s2_in, s2_ref),
            c_ref if first else c_in,
        )
        if not first:
            c_ref[...] = c_in[...]

    operands = [place, *payloads, w] + ([] if first else list(state))
    aliases = {} if first else {2 + count + i: i for i in range(4)}
    return pl.pallas_call(
        body,
        out_shape=state_shapes(sz),
        in_specs=[SM] + [VM] * (len(operands) - 1),
        out_specs=[VM] * 4,
        scratch_shapes=[pltpu.VMEM((sz.work_rows, count * sz.width), jnp.bfloat16)],
        input_output_aliases=aliases,
        compiler_params=PARAMS,
        cost_estimate=pl.CostEstimate(
            flops=1_000_000_000 * count, transcendentals=0, bytes_accessed=1_000_000
        ),
        name=name,
    )(*operands)


def last_shard(sz, place, top, bottom, w, q_gain, k_gain, state):
    far = sz.peers // 2
    heads = sz.cols // sz.head_dim

    def body(place_ref, top_ref, bottom_ref, w_ref, q_gain_ref, k_gain_ref, y_in, s1_in, s2_in, c_in, att_ref, *scratch):
        mod_ref, whole_ref, y_ref, s1_ref, s2_ref, *rest = scratch
        whole_ref[0 : sz.cut, :] = top_ref[...]
        whole_ref[sz.cut :, :] = bottom_ref[...]
        accumulate(
            sz,
            place_ref,
            [(far, whole_ref)],
            w_ref,
            mod_ref,
            (y_in, y_ref),
            (s1_in, s1_ref),
            (s2_in, s2_ref),
            c_in,
        )
        attend(sz, q_gain_ref, k_gain_ref, y_ref, s1_ref, s2_ref, *rest, att_ref)

    operands = [place, top, bottom, w, q_gain, k_gain, *state]
    bf16, f32 = jnp.bfloat16, jnp.float32
    return pl.pallas_call(
        body,
        out_shape=jax.ShapeDtypeStruct((sz.slots * sz.image_len, sz.cols), bf16),
        in_specs=[SM] + [VM] * (len(operands) - 1),
        out_specs=VM,
        scratch_shapes=[
            pltpu.VMEM((sz.work_rows, sz.width), bf16),
            pltpu.VMEM((sz.payload, sz.width), bf16),
            pltpu.VMEM((3, sz.work_rows, sz.cols), f32),
            pltpu.VMEM((sz.token_rows, 128), f32),
            pltpu.VMEM((sz.token_rows, 128), f32),
            pltpu.VMEM((sz.token_rows, 128), f32),
            pltpu.VMEM((sz.token_rows, 128), f32),
            pltpu.VMEM((sz.slots, sz.image_len, sz.cols), bf16),
            pltpu.VMEM((sz.slots, heads * sz.seq, sz.cols), bf16),
            pltpu.VMEM((sz.slots, heads * sz.seq, sz.cols), bf16),
            pltpu.VMEM((heads * sz.seq, sz.cols), bf16),
            pltpu.VMEM((sz.slots, sz.image_len, heads * sz.seq), f32),
        ],
        compiler_params=PARAMS,
        cost_estimate=pl.CostEstimate(flops=6_000_000_000, transcendentals=0, bytes_accessed=1_000_000),
        name="attend",
    )(*operands)


def send_parts(sz, place, offsets, gates, w_out, coef, att, name):
    count = len(offsets)

    def body(place_ref, coef_ref, w_out_ref, att_ref, *refs):
        rows = [
            ref[at : at + sz.mod_rows, :].astype(jnp.float32)
            for ref, (_, at) in zip(refs[:count], gates)
        ]
        project_out(sz, place_ref, offsets, rows, w_out_ref, coef_ref, att_ref, refs[count:])

    return pl.pallas_call(
        body,
        out_shape=[jax.ShapeDtypeStruct((sz.image_rows, sz.width), jnp.bfloat16)] * count,
        in_specs=[SM, SM] + [VM] * (2 + count),
        out_specs=[VM] * count,
        compiler_params=PARAMS,
        cost_estimate=pl.CostEstimate(flops=300_000_000 * count, transcendentals=0, bytes_accessed=1_000_000),
        name=name,
    )(place, coef, w_out, att, *[array for array, _ in gates])


def on_device(
    image_latents,
    text_states,
    modulation,
    w_qkv,
    w_out,
    q_gain,
    k_gain,
    branch_count,
    branch_sign,
    guide_weight,
):
    images, image_len, width = image_latents.shape
    slots, text_len, _ = text_states.shape
    peers = lax.axis_size("mp")
    sz = Sizes(images, image_len, slots, text_len, width, peers, q_gain.shape[0], w_out.shape[0])

    modulation_rows = jnp.pad(
        jnp.transpose(modulation, (1, 0, 2)), ((0, 0), (0, sz.mod_rows - slots), (0, 0))
    )
    payload = jnp.concatenate(
        [
            image_latents.reshape(sz.image_rows, width),
            text_states.reshape(slots * text_len, width),
            modulation_rows.reshape(3 * sz.mod_rows, width),
        ],
        axis=0,
    )
    w = jnp.transpose(w_qkv, (1, 0, 2))
    place = (lax.axis_index("mp") + jnp.arange(peers, dtype=jnp.int32)) % peers

    is_live = (jnp.arange(sz.per_image, dtype=jnp.int32)[None, :] < branch_count[:, None]).reshape(-1)
    weights_live = jnp.where(is_live, guide_weight, 0).astype(jnp.float32)
    weight_total = jnp.sum(weights_live.reshape(images, sz.per_image), axis=1)
    coef = (2 * branch_sign - 1).astype(jnp.float32) * weights_live / jnp.repeat(weight_total, sz.per_image)
    coef_total = jnp.sum(coef.reshape(images, sz.per_image), axis=1)

    def shifted(x, by):
        return lax.ppermute(x, "mp", [(i, (i + by) % peers) for i in range(peers)])

    far = peers // 2
    ring = {0: payload}
    below = above = payload
    state = None
    for step in range(1, far):
        below, above = shifted(below, 1), shifted(above, -1)
        offsets = [0] if step == 1 else [peers - step + 1, step - 1]
        state = add_shards(sz, place, offsets, [ring[o] for o in offsets], w, state, f"project_{step}")
        ring[peers - step], ring[step] = below, above
        below, above, state = lax.optimization_barrier((below, above, state))
    top, bottom = shifted(below[: sz.cut], 1), shifted(above[sz.cut :], -1)
    offsets = [far + 1, far - 1]
    state = add_shards(sz, place, offsets, [ring[o] for o in offsets], w, state, f"project_{far}")
    top, bottom, state = lax.optimization_barrier((top, bottom, state))
    att = last_shard(
        sz, place, top, bottom, w, q_gain.reshape(1, -1), k_gain.reshape(1, -1), state
    )
    gates = {o: (array, sz.gate_at) for o, array in ring.items()}
    gates[far] = (bottom, sz.gate_at - sz.cut)
    parts = {}
    early = [far, far + 1, far - 1]
    late = [o for d in range(far - 2, 0, -1) for o in (d, peers - d)] + [0]
    for name, group in (("parts_far", early), ("parts_near", late)):
        made = send_parts(sz, place, group, [gates[o] for o in group], w_out, coef, att, name)
        for offset, part in zip(group, made):
            parts[offset] = shifted(part, offset) if offset else part
    total = parts[0].astype(jnp.float32)
    for offset in early + late[:-1]:
        total = total + parts[offset].astype(jnp.float32)
    total = total.reshape(images, image_len, width)
    return (image_latents.astype(jnp.float32) * coef_total[:, None, None] + total).astype(jnp.bfloat16)


def solution(mesh):
    placed = (
        P("dp", None, "mp"),
        P("dp", None, "mp"),
        P("dp", None, "mp"),
        P(None, None, "mp"),
        P("mp", None),
        P(),
        P(),
        P("dp"),
        P("dp"),
        P("dp"),
    )
    return jax.shard_map(
        on_device, mesh=mesh, in_specs=placed, out_specs=P("dp", None, "mp"), check_vma=False
    )
```

```python
import jax
import jax.numpy as jnp
from jax import lax
from jax.experimental import pallas as pl
from jax.experimental.pallas import tpu as pltpu
from jax.sharding import PartitionSpec as P

epsilon = 1e-06
ROUND = 16


def up(rows):
    return -(-rows // ROUND) * ROUND


class Sizes:
    def __init__(self, images, image_len, slots, text_len, width, peers, head_dim, local_cols):
        self.images, self.image_len, self.slots, self.text_len = images, image_len, slots, text_len
        self.width, self.peers, self.head_dim, self.cols = width, peers, head_dim, local_cols
        self.per_image = slots // images
        self.seq = image_len + text_len
        self.image_rows = images * image_len
        self.token_rows = self.image_rows + slots * text_len
        self.mod_rows = up(slots + 1)
        self.shift_at = self.token_rows
        self.scale_at = self.shift_at + self.mod_rows
        self.gate_at = self.scale_at + self.mod_rows
        self.payload = self.gate_at + self.mod_rows
        self.cut = up(self.payload // 2)
        self.seq_rows = slots * self.seq
        self.work_rows = self.seq_rows + 2 * self.mod_rows


def accumulate(sz, place_ref, shards, w_ref, mod_ref, y_refs, s1_refs, s2_refs, c_ref):
    width, lanes = sz.width, 128
    (y_in, y_ref), (s1_in, s1_ref), (s2_in, s2_ref) = y_refs, s1_refs, s2_refs
    first = y_in is None
    s1 = None
    for at, (offset, payload) in enumerate(shards):
        tokens = payload[0 : sz.token_rows, :].astype(jnp.float32)
        if first and at == 0:
            center = jnp.broadcast_to(
                jnp.sum(tokens, axis=1, keepdims=True) * (1.0 / width), (sz.token_rows, lanes)
            )
            c_ref[...] = center
        elif at == 0:
            center = c_ref[...]
        tokens = tokens - jnp.concatenate([center] * (width // lanes), axis=1)
        squares = tokens * tokens
        for part in range(width // lanes):
            piece = tokens[:, part * lanes : (part + 1) * lanes]
            piece2 = squares[:, part * lanes : (part + 1) * lanes]
            if s1 is None:
                s1, s2 = piece, piece2
            else:
                s1, s2 = s1 + piece, s2 + piece2
        cols = slice(at * width, (at + 1) * width)
        scale = payload[sz.scale_at : sz.scale_at + sz.mod_rows, :].astype(jnp.float32)
        row = lax.broadcasted_iota(jnp.int32, scale.shape, 0)
        scale_one = jnp.where(row == sz.slots, 1.0, scale)
        for s in range(sz.slots):
            image = s // sz.per_image
            factor = 1.0 + scale[s : s + 1, :]
            picture = tokens[image * sz.image_len : (image + 1) * sz.image_len, :]
            text_at = sz.image_rows + s * sz.text_len
            text = tokens[text_at : text_at + sz.text_len, :]
            base = s * sz.seq
            mod_ref[base : base + sz.image_len, cols] = (picture * factor).astype(jnp.bfloat16)
            mod_ref[base + sz.image_len : base + sz.seq, cols] = (text * factor).astype(jnp.bfloat16)
        mod_ref[sz.seq_rows : sz.seq_rows + sz.mod_rows, cols] = scale_one.astype(jnp.bfloat16)
        mod_ref[sz.seq_rows + sz.mod_rows : sz.work_rows, cols] = payload[
            sz.shift_at : sz.shift_at + sz.mod_rows, :
        ]
    if first:
        s1_ref[...] = s1
        s2_ref[...] = s2
    else:
        s1_ref[...] = s1_in[...] + s1
        s2_ref[...] = s2_in[...] + s2
    for third in range(3):
        weights = jnp.concatenate(
            [
                w_ref[third, pl.ds(pl.multiple_of(place_ref[offset] * width, 128), width), :]
                for offset, _ in shards
            ],
            axis=0,
        )
        part = jnp.dot(
            mod_ref[:, 0 : len(shards) * width], weights, preferred_element_type=jnp.float32
        )
        if first:
            y_ref[third] = part
        else:
            y_ref[third] = y_in[third] + part


def rms_norm(values, gain):
    return values * lax.rsqrt(jnp.mean(values * values, axis=-1, keepdims=True) + epsilon) * gain


def attend(sz, q_gain_ref, k_gain_ref, y_ref, s1_ref, s2_ref, rb_ref, mb_ref, q_ref, k_ref, v_ref, sums_ref, scores_ref, att_ref):
    full = float(sz.width * sz.peers)
    dim, heads, seq, pic = sz.head_dim, sz.cols // sz.head_dim, sz.seq, sz.image_len
    mean = jnp.sum(s1_ref[...], axis=1, keepdims=True) * (1.0 / full)
    second = jnp.sum(s2_ref[...], axis=1, keepdims=True) * (1.0 / full)
    rstd = lax.rsqrt(jnp.maximum(second - mean * mean, 0.0) + epsilon)
    rb_ref[...] = jnp.broadcast_to(rstd, (sz.token_rows, 128))
    mb_ref[...] = jnp.broadcast_to(-mean * rstd, (sz.token_rows, 128))
    q_gain, k_gain = q_gain_ref[...], k_gain_ref[...]
    ones_at = sz.seq_rows + sz.slots
    zeros = jnp.zeros((seq, dim), jnp.bfloat16)
    ones = jnp.ones((seq, dim), jnp.bfloat16)
    for h in range(heads):
        for g in range(heads):
            sums_ref[h * seq : (h + 1) * seq, g * dim : (g + 1) * dim] = ones if g == h else zeros
    for s in range(sz.slots):
        image = s // sz.per_image
        text_at = sz.image_rows + s * sz.text_len
        scale_at, shift_at, base = sz.seq_rows + s, sz.seq_rows + sz.mod_rows + s, s * seq
        spans = [
            (0, pic, image * pic),
            (pic, seq, text_at),
        ]
        for h in range(heads):
            cs = slice(h * dim, (h + 1) * dim)
            for third in range(3):
                u = y_ref[third, scale_at : scale_at + 1, cs] + y_ref[third, ones_at : ones_at + 1, cs]
                v = y_ref[third, shift_at : shift_at + 1, cs]
                for lo, hi, at in spans[: 1 if third == 0 else 2]:
                    rows = slice(at, at + hi - lo)
                    value = y_ref[third, base + lo : base + hi, cs] * rb_ref[rows, :]
                    value = value + (mb_ref[rows, :] * u + v)
                    if third == 0:
                        q_ref[s, :, cs] = rms_norm(value, q_gain).astype(jnp.bfloat16)
                    else:
                        if third == 1:
                            value = rms_norm(value, k_gain)
                        out = k_ref if third == 1 else v_ref
                        out[s, h * seq + lo : h * seq + hi, cs] = value.astype(jnp.bfloat16)
            for g in range(heads):
                if g != h:
                    k_ref[s, h * seq : (h + 1) * seq, g * dim : (g + 1) * dim] = zeros
                    v_ref[s, h * seq : (h + 1) * seq, g * dim : (g + 1) * dim] = zeros
    for s in range(sz.slots):
        scores_ref[s] = lax.dot_general(
            q_ref[s], k_ref[s], (((1,), (1,)), ((), ())), preferred_element_type=jnp.float32
        ) * dim ** (-0.5)
    lane = lax.broadcasted_iota(jnp.int32, (pic, heads * seq), 1)
    sums_rhs = sums_ref[...]
    for s in range(sz.slots):
        scores = scores_ref[s]
        top = None
        for h in range(heads):
            mine = (lane >= h * seq) & (lane < (h + 1) * seq)
            peak = jnp.max(jnp.where(mine, scores, -jnp.inf), axis=1, keepdims=True)
            top = jnp.broadcast_to(peak, scores.shape) if top is None else jnp.where(mine, peak, top)
        e = jnp.exp(scores - top).astype(jnp.bfloat16)
        total = jnp.dot(e, sums_rhs, preferred_element_type=jnp.float32)
        mixed = jnp.dot(e, v_ref[s], preferred_element_type=jnp.float32)
        att_ref[s * pic : (s + 1) * pic, :] = (mixed / total).astype(jnp.bfloat16)


def project_out(sz, place_ref, offsets, gate_rows, w_out_ref, coef_ref, att_ref, out_refs):
    for offset, gates, out_ref in zip(offsets, gate_rows, out_refs):
        cols = pl.ds(pl.multiple_of(place_ref[offset] * sz.width, 128), sz.width)
        rows = jnp.dot(att_ref[...], w_out_ref[:, cols], preferred_element_type=jnp.float32)
        for image in range(sz.images):
            total = None
            for s in range(image * sz.per_image, (image + 1) * sz.per_image):
                term = rows[s * sz.image_len : (s + 1) * sz.image_len, :] * (
                    gates[s : s + 1, :] * coef_ref[s]
                )
                total = term if total is None else total + term
            out_ref[image * sz.image_len : (image + 1) * sz.image_len, :] = total.astype(jnp.bfloat16)


VM = pl.BlockSpec(memory_space=pltpu.VMEM)
SM = pl.BlockSpec(memory_space=pltpu.SMEM)
PARAMS = pltpu.CompilerParams(vmem_limit_bytes=40 * 1024 * 1024)


def state_shapes(sz):
    f32 = jnp.float32
    return [
        jax.ShapeDtypeStruct((3, sz.work_rows, sz.cols), f32),
        jax.ShapeDtypeStruct((sz.token_rows, 128), f32),
        jax.ShapeDtypeStruct((sz.token_rows, 128), f32),
        jax.ShapeDtypeStruct((sz.token_rows, 128), f32),
    ]


def add_shards(sz, place, offsets, payloads, w, state, name):
    first = state is None
    count = len(offsets)

    def body(place_ref, *refs):
        payload_refs, refs = refs[:count], refs[count:]
        w_ref, refs = refs[0], refs[1:]
        y_in, s1_in, s2_in, c_in = (None, None, None, refs[3]) if first else refs[:4]
        if not first:
            refs = refs[4:]
        y_ref, s1_ref, s2_ref, c_ref, mod_ref = refs
        accumulate(
            sz,
            place_ref,
            list(zip(offsets, payload_refs)),
            w_ref,
            mod_ref,
            (y_in, y_ref),
            (s1_in, s1_ref),
            (s2_in, s2_ref),
            c_ref if first else c_in,
        )
        if not first:
            c_ref[...] = c_in[...]

    operands = [place, *payloads, w] + ([] if first else list(state))
    aliases = {} if first else {2 + count + i: i for i in range(4)}
    return pl.pallas_call(
        body,
        out_shape=state_shapes(sz),
        in_specs=[SM] + [VM] * (len(operands) - 1),
        out_specs=[VM] * 4,
        scratch_shapes=[pltpu.VMEM((sz.work_rows, count * sz.width), jnp.bfloat16)],
        input_output_aliases=aliases,
        compiler_params=PARAMS,
        cost_estimate=pl.CostEstimate(
            flops=1_000_000_000 * count, transcendentals=0, bytes_accessed=1_000_000
        ),
        name=name,
    )(*operands)


def pack(sz, image_latents, text_states, modulation):
    def body(image_hbm, text_hbm, mod_hbm, out_ref, mod_ref, sems):
        copies = [
            pltpu.make_async_copy(mod_hbm, mod_ref, sems.at[0]),
            pltpu.make_async_copy(image_hbm, out_ref.at[0 : sz.image_rows, :], sems.at[1]),
            pltpu.make_async_copy(
                text_hbm, out_ref.at[sz.image_rows : sz.token_rows, :], sems.at[2]
            ),
        ]
        for copy in copies:
            copy.start()
        copies[0].wait()
        for part in range(3):
            at = sz.shift_at + part * sz.mod_rows
            rows = jnp.concatenate(
                [mod_ref[part], jnp.zeros((sz.mod_rows - sz.slots, sz.width), jnp.bfloat16)], axis=0
            )
            out_ref[at : at + sz.mod_rows, :] = rows
        copies[1].wait()
        copies[2].wait()

    return pl.pallas_call(
        body,
        out_shape=jax.ShapeDtypeStruct((sz.payload, sz.width), jnp.bfloat16),
        in_specs=[pl.BlockSpec(memory_space=pl.ANY)] * 3,
        out_specs=VM,
        scratch_shapes=[
            pltpu.VMEM((3, sz.slots, sz.width), jnp.bfloat16),
            pltpu.SemaphoreType.DMA((3,)),
        ],
        compiler_params=PARAMS,
        name="pack",
    )(
        image_latents.reshape(sz.image_rows, sz.width),
        text_states.reshape(sz.slots * sz.text_len, sz.width),
        jnp.transpose(modulation, (1, 0, 2)),
    )


def last_shard(sz, place, ring, top, bottom, w, w_out, coef, q_gain, k_gain, state):
    far = sz.peers // 2
    heads = sz.cols // sz.head_dim
    near = [o for o in range(sz.peers) if o != far]
    n_near = len(near)

    def body(place_ref, coef_ref, top_ref, bottom_ref, w_ref, w_out_ref, q_gain_ref, k_gain_ref, y_in, s1_in, s2_in, c_in, *refs):
        payloads, refs = refs[:n_near], refs[n_near:]
        out_refs, (att_ref, mod_ref, whole_ref, y_ref, s1_ref, s2_ref, *rest) = refs[: sz.peers], refs[sz.peers :]
        whole_ref[0 : sz.cut, :] = top_ref[...]
        whole_ref[sz.cut :, :] = bottom_ref[...]
        accumulate(
            sz,
            place_ref,
            [(far, whole_ref)],
            w_ref,
            mod_ref,
            (y_in, y_ref),
            (s1_in, s1_ref),
            (s2_in, s2_ref),
            c_in,
        )
        attend(sz, q_gain_ref, k_gain_ref, y_ref, s1_ref, s2_ref, *rest, att_ref)
        sources = dict(zip(near, payloads))
        sources[far] = whole_ref
        gates = [
            sources[o][sz.gate_at : sz.gate_at + sz.mod_rows, :].astype(jnp.float32)
            for o in range(sz.peers)
        ]
        project_out(sz, place_ref, range(sz.peers), gates, w_out_ref, coef_ref, att_ref, out_refs)

    operands = [place, coef, top, bottom, w, w_out, q_gain, k_gain, *state, *[ring[o] for o in near]]
    bf16, f32 = jnp.bfloat16, jnp.float32
    return pl.pallas_call(
        body,
        out_shape=[jax.ShapeDtypeStruct((sz.image_rows, sz.width), bf16)] * sz.peers,
        in_specs=[SM, SM] + [VM] * (len(operands) - 2),
        out_specs=[VM] * sz.peers,
        scratch_shapes=[
            pltpu.VMEM((sz.slots * sz.image_len, sz.cols), bf16),
            pltpu.VMEM((sz.work_rows, sz.width), bf16),
            pltpu.VMEM((sz.payload, sz.width), bf16),
            pltpu.VMEM((3, sz.work_rows, sz.cols), f32),
            pltpu.VMEM((sz.token_rows, 128), f32),
            pltpu.VMEM((sz.token_rows, 128), f32),
            pltpu.VMEM((sz.token_rows, 128), f32),
            pltpu.VMEM((sz.token_rows, 128), f32),
            pltpu.VMEM((sz.slots, sz.image_len, sz.cols), bf16),
            pltpu.VMEM((sz.slots, heads * sz.seq, sz.cols), bf16),
            pltpu.VMEM((sz.slots, heads * sz.seq, sz.cols), bf16),
            pltpu.VMEM((heads * sz.seq, sz.cols), bf16),
            pltpu.VMEM((sz.slots, sz.image_len, heads * sz.seq), f32),
        ],
        compiler_params=PARAMS,
        cost_estimate=pl.CostEstimate(flops=9_000_000_000, transcendentals=0, bytes_accessed=1_000_000),
        name="attend",
    )(*operands)


def on_device(
    image_latents,
    text_states,
    modulation,
    w_qkv,
    w_out,
    q_gain,
    k_gain,
    branch_count,
    branch_sign,
    guide_weight,
):
    images, image_len, width = image_latents.shape
    slots, text_len, _ = text_states.shape
    peers = lax.axis_size("mp")
    sz = Sizes(images, image_len, slots, text_len, width, peers, q_gain.shape[0], w_out.shape[0])

    payload = pack(sz, image_latents, text_states, modulation)
    w = jnp.transpose(w_qkv, (1, 0, 2))
    place = (lax.axis_index("mp") + jnp.arange(peers, dtype=jnp.int32)) % peers

    is_live = (jnp.arange(sz.per_image, dtype=jnp.int32)[None, :] < branch_count[:, None]).reshape(-1)
    weights_live = jnp.where(is_live, guide_weight, 0).astype(jnp.float32)
    weight_total = jnp.sum(weights_live.reshape(images, sz.per_image), axis=1)
    coef = (2 * branch_sign - 1).astype(jnp.float32) * weights_live / jnp.repeat(weight_total, sz.per_image)
    coef_total = jnp.sum(coef.reshape(images, sz.per_image), axis=1)

    def shifted(x, by):
        return lax.ppermute(x, "mp", [(i, (i + by) % peers) for i in range(peers)])

    far = peers // 2
    ring = {0: payload}
    below = above = payload
    state = None
    for step in range(1, far):
        below, above = shifted(below, 1), shifted(above, -1)
        offsets = [0] if step == 1 else [peers - step + 1, step - 1]
        state = add_shards(sz, place, offsets, [ring[o] for o in offsets], w, state, f"project_{step}")
        ring[peers - step], ring[step] = below, above
        below, above, state = lax.optimization_barrier((below, above, state))
    top, bottom = shifted(below[: sz.cut], 1), shifted(above[sz.cut :], -1)
    offsets = [far + 1, far - 1]
    state = add_shards(sz, place, offsets, [ring[o] for o in offsets], w, state, f"project_{far}")
    top, bottom, state = lax.optimization_barrier((top, bottom, state))
    parts = last_shard(
        sz,
        place,
        ring,
        top,
        bottom,
        w,
        w_out,
        coef,
        q_gain.reshape(1, -1),
        k_gain.reshape(1, -1),
        state,
    )
    total = parts[0].astype(jnp.float32)
    for offset in [far] + [o for d in range(far - 1, 0, -1) for o in (peers - d, d)]:
        total = total + shifted(parts[offset], offset).astype(jnp.float32)
    total = total.reshape(images, image_len, width)
    return (image_latents.astype(jnp.float32) * coef_total[:, None, None] + total).astype(jnp.bfloat16)


def solution(mesh):
    placed = (
        P("dp", None, "mp"),
        P("dp", None, "mp"),
        P("dp", None, "mp"),
        P(None, None, "mp"),
        P("mp", None),
        P(),
        P(),
        P("dp"),
        P("dp"),
        P("dp"),
    )
    return jax.shard_map(
        on_device, mesh=mesh, in_specs=placed, out_specs=P("dp", None, "mp"), check_vma=False
    )
```

```python
import jax
import jax.numpy as jnp
from jax import lax
from jax.experimental import pallas as pl
from jax.experimental.pallas import tpu as pltpu
from jax.sharding import PartitionSpec as P

epsilon = 1e-06
ROUND = 16


def up(rows):
    return -(-rows // ROUND) * ROUND


class Sizes:
    def __init__(self, images, image_len, slots, text_len, width, peers, head_dim, local_cols):
        self.images, self.image_len, self.slots, self.text_len = images, image_len, slots, text_len
        self.width, self.peers, self.head_dim, self.cols = width, peers, head_dim, local_cols
        self.per_image = slots // images
        self.seq = image_len + text_len
        self.image_rows = images * image_len
        self.token_rows = self.image_rows + slots * text_len
        self.mod_rows = up(slots + 1)
        self.shift_at = self.token_rows
        self.scale_at = self.shift_at + self.mod_rows
        self.gate_at = self.scale_at + self.mod_rows
        self.payload = self.gate_at + self.mod_rows
        self.cut = up(self.payload // 2)
        self.seq_rows = slots * self.seq
        self.work_rows = self.seq_rows + 2 * self.mod_rows


def accumulate(sz, place_ref, shards, w_ref, mod_ref, y_refs, s1_refs, s2_refs, c_ref):
    width, lanes = sz.width, 128
    (y_in, y_ref), (s1_in, s1_ref), (s2_in, s2_ref) = y_refs, s1_refs, s2_refs
    first = y_in is None
    s1 = None
    for at, (offset, payload) in enumerate(shards):
        tokens = payload[0 : sz.token_rows, :].astype(jnp.float32)
        if first and at == 0:
            center = jnp.broadcast_to(
                jnp.sum(tokens, axis=1, keepdims=True) * (1.0 / width), (sz.token_rows, lanes)
            )
            c_ref[...] = center
        elif at == 0:
            center = c_ref[...]
        tokens = tokens - jnp.concatenate([center] * (width // lanes), axis=1)
        squares = tokens * tokens
        for part in range(width // lanes):
            piece = tokens[:, part * lanes : (part + 1) * lanes]
            piece2 = squares[:, part * lanes : (part + 1) * lanes]
            if s1 is None:
                s1, s2 = piece, piece2
            else:
                s1, s2 = s1 + piece, s2 + piece2
        cols = slice(at * width, (at + 1) * width)
        scale = payload[sz.scale_at : sz.scale_at + sz.mod_rows, :].astype(jnp.float32)
        row = lax.broadcasted_iota(jnp.int32, scale.shape, 0)
        scale_one = jnp.where(row == sz.slots, 1.0, scale)
        for s in range(sz.slots):
            image = s // sz.per_image
            factor = 1.0 + scale[s : s + 1, :]
            picture = tokens[image * sz.image_len : (image + 1) * sz.image_len, :]
            text_at = sz.image_rows + s * sz.text_len
            text = tokens[text_at : text_at + sz.text_len, :]
            base = s * sz.seq
            mod_ref[base : base + sz.image_len, cols] = (picture * factor).astype(jnp.bfloat16)
            mod_ref[base + sz.image_len : base + sz.seq, cols] = (text * factor).astype(jnp.bfloat16)
        mod_ref[sz.seq_rows : sz.seq_rows + sz.mod_rows, cols] = scale_one.astype(jnp.bfloat16)
        mod_ref[sz.seq_rows + sz.mod_rows : sz.work_rows, cols] = payload[
            sz.shift_at : sz.shift_at + sz.mod_rows, :
        ]
    if first:
        s1_ref[...] = s1
        s2_ref[...] = s2
    else:
        s1_ref[...] = s1_in[...] + s1
        s2_ref[...] = s2_in[...] + s2
    for third in range(3):
        weights = jnp.concatenate(
            [
                w_ref[third, pl.ds(pl.multiple_of(place_ref[offset] * width, 128), width), :]
                for offset, _ in shards
            ],
            axis=0,
        )
        part = jnp.dot(
            mod_ref[:, 0 : len(shards) * width], weights, preferred_element_type=jnp.float32
        )
        if first:
            y_ref[third] = part
        else:
            y_ref[third] = y_in[third] + part


def rms_norm(values, gain):
    return values * lax.rsqrt(jnp.mean(values * values, axis=-1, keepdims=True) + epsilon) * gain


def attend(sz, q_gain_ref, k_gain_ref, y_ref, s1_ref, s2_ref, rb_ref, mb_ref, q_ref, k_ref, v_ref, sums_ref, scores_ref, att_ref):
    full = float(sz.width * sz.peers)
    dim, heads, seq, pic = sz.head_dim, sz.cols // sz.head_dim, sz.seq, sz.image_len
    mean = jnp.sum(s1_ref[...], axis=1, keepdims=True) * (1.0 / full)
    second = jnp.sum(s2_ref[...], axis=1, keepdims=True) * (1.0 / full)
    rstd = lax.rsqrt(jnp.maximum(second - mean * mean, 0.0) + epsilon)
    rb_ref[...] = jnp.broadcast_to(rstd, (sz.token_rows, 128))
    mb_ref[...] = jnp.broadcast_to(-mean * rstd, (sz.token_rows, 128))
    q_gain, k_gain = q_gain_ref[...], k_gain_ref[...]
    ones_at = sz.seq_rows + sz.slots
    zeros = jnp.zeros((seq, dim), jnp.bfloat16)
    ones = jnp.ones((seq, dim), jnp.bfloat16)
    for h in range(heads):
        for g in range(heads):
            sums_ref[h * seq : (h + 1) * seq, g * dim : (g + 1) * dim] = ones if g == h else zeros
    for s in range(sz.slots):
        image = s // sz.per_image
        text_at = sz.image_rows + s * sz.text_len
        scale_at, shift_at, base = sz.seq_rows + s, sz.seq_rows + sz.mod_rows + s, s * seq
        spans = [
            (0, pic, image * pic),
            (pic, seq, text_at),
        ]
        for h in range(heads):
            cs = slice(h * dim, (h + 1) * dim)
            for third in range(3):
                u = y_ref[third, scale_at : scale_at + 1, cs] + y_ref[third, ones_at : ones_at + 1, cs]
                v = y_ref[third, shift_at : shift_at + 1, cs]
                for lo, hi, at in spans[: 1 if third == 0 else 2]:
                    rows = slice(at, at + hi - lo)
                    value = y_ref[third, base + lo : base + hi, cs] * rb_ref[rows, :]
                    value = value + (mb_ref[rows, :] * u + v)
                    if third == 0:
                        q_ref[s, :, cs] = rms_norm(value, q_gain).astype(jnp.bfloat16)
                    else:
                        if third == 1:
                            value = rms_norm(value, k_gain)
                        out = k_ref if third == 1 else v_ref
                        out[s, h * seq + lo : h * seq + hi, cs] = value.astype(jnp.bfloat16)
            for g in range(heads):
                if g != h:
                    k_ref[s, h * seq : (h + 1) * seq, g * dim : (g + 1) * dim] = zeros
                    v_ref[s, h * seq : (h + 1) * seq, g * dim : (g + 1) * dim] = zeros
    for s in range(sz.slots):
        scores_ref[s] = lax.dot_general(
            q_ref[s], k_ref[s], (((1,), (1,)), ((), ())), preferred_element_type=jnp.float32
        ) * dim ** (-0.5)
    lane = lax.broadcasted_iota(jnp.int32, (pic, heads * seq), 1)
    sums_rhs = sums_ref[...]
    for s in range(sz.slots):
        scores = scores_ref[s]
        top = None
        for h in range(heads):
            mine = (lane >= h * seq) & (lane < (h + 1) * seq)
            peak = jnp.max(jnp.where(mine, scores, -jnp.inf), axis=1, keepdims=True)
            top = jnp.broadcast_to(peak, scores.shape) if top is None else jnp.where(mine, peak, top)
        e = jnp.exp(scores - top).astype(jnp.bfloat16)
        total = jnp.dot(e, sums_rhs, preferred_element_type=jnp.float32)
        mixed = jnp.dot(e, v_ref[s], preferred_element_type=jnp.float32)
        att_ref[s * pic : (s + 1) * pic, :] = (mixed / total).astype(jnp.bfloat16)


def project_out(sz, place_ref, offsets, gate_rows, w_out_ref, coef_ref, att_ref, out_refs):
    for offset, gates, out_ref in zip(offsets, gate_rows, out_refs):
        cols = pl.ds(pl.multiple_of(place_ref[offset] * sz.width, 128), sz.width)
        rows = jnp.dot(att_ref[...], w_out_ref[:, cols], preferred_element_type=jnp.float32)
        for image in range(sz.images):
            total = None
            for s in range(image * sz.per_image, (image + 1) * sz.per_image):
                term = rows[s * sz.image_len : (s + 1) * sz.image_len, :] * (
                    gates[s : s + 1, :] * coef_ref[s]
                )
                total = term if total is None else total + term
            out_ref[image * sz.image_len : (image + 1) * sz.image_len, :] = total.astype(jnp.bfloat16)


VM = pl.BlockSpec(memory_space=pltpu.VMEM)
SM = pl.BlockSpec(memory_space=pltpu.SMEM)
PARAMS = pltpu.CompilerParams(vmem_limit_bytes=40 * 1024 * 1024)


def state_shapes(sz):
    f32 = jnp.float32
    return [
        jax.ShapeDtypeStruct((3, sz.work_rows, sz.cols), f32),
        jax.ShapeDtypeStruct((sz.token_rows, 128), f32),
        jax.ShapeDtypeStruct((sz.token_rows, 128), f32),
        jax.ShapeDtypeStruct((sz.token_rows, 128), f32),
    ]


def add_shards(sz, place, offsets, payloads, w, state, name):
    first = state is None
    count = len(offsets)

    def body(place_ref, *refs):
        payload_refs, refs = refs[:count], refs[count:]
        w_ref, refs = refs[0], refs[1:]
        y_in, s1_in, s2_in, c_in = (None, None, None, refs[3]) if first else refs[:4]
        if not first:
            refs = refs[4:]
        y_ref, s1_ref, s2_ref, c_ref, gate_ref, mod_ref = refs
        accumulate(
            sz,
            place_ref,
            list(zip(offsets, payload_refs)),
            w_ref,
            mod_ref,
            (y_in, y_ref),
            (s1_in, s1_ref),
            (s2_in, s2_ref),
            c_ref if first else c_in,
        )
        if not first:
            c_ref[...] = c_in[...]
        for at, payload in enumerate(payload_refs):
            gate_ref[at] = payload[sz.gate_at : sz.gate_at + sz.mod_rows, :]

    operands = [place, *payloads, w] + ([] if first else list(state))
    aliases = {} if first else {2 + count + i: i for i in range(4)}
    gate_shape = jax.ShapeDtypeStruct((count, sz.mod_rows, sz.width), jnp.bfloat16)
    *state, gates = pl.pallas_call(
        body,
        out_shape=state_shapes(sz) + [gate_shape],
        in_specs=[SM] + [VM] * (len(operands) - 1),
        out_specs=[VM] * 5,
        scratch_shapes=[pltpu.VMEM((sz.work_rows, count * sz.width), jnp.bfloat16)],
        input_output_aliases=aliases,
        compiler_params=PARAMS,
        cost_estimate=pl.CostEstimate(
            flops=1_000_000_000 * count, transcendentals=0, bytes_accessed=1_000_000
        ),
        name=name,
    )(*operands)
    return state, gates


def pack(sz, image_latents, text_states, modulation):
    def body(image_hbm, text_hbm, mod_hbm, out_ref, mod_ref, sems):
        copies = [
            pltpu.make_async_copy(mod_hbm, mod_ref, sems.at[0]),
            pltpu.make_async_copy(image_hbm, out_ref.at[0 : sz.image_rows, :], sems.at[1]),
            pltpu.make_async_copy(
                text_hbm, out_ref.at[sz.image_rows : sz.token_rows, :], sems.at[2]
            ),
        ]
        for copy in copies:
            copy.start()
        copies[0].wait()
        for part in range(3):
            at = sz.shift_at + part * sz.mod_rows
            rows = jnp.concatenate(
                [mod_ref[part], jnp.zeros((sz.mod_rows - sz.slots, sz.width), jnp.bfloat16)], axis=0
            )
            out_ref[at : at + sz.mod_rows, :] = rows
        copies[1].wait()
        copies[2].wait()

    return pl.pallas_call(
        body,
        out_shape=jax.ShapeDtypeStruct((sz.payload, sz.width), jnp.bfloat16),
        in_specs=[pl.BlockSpec(memory_space=pltpu.HBM)] * 3,
        out_specs=VM,
        scratch_shapes=[
            pltpu.VMEM((3, sz.slots, sz.width), jnp.bfloat16),
            pltpu.SemaphoreType.DMA((3,)),
        ],
        compiler_params=PARAMS,
        name="pack",
    )(
        *[
            pltpu.with_memory_space_constraint(x, pltpu.HBM)
            for x in (
                image_latents.reshape(sz.image_rows, sz.width),
                text_states.reshape(sz.slots * sz.text_len, sz.width),
                jnp.transpose(modulation, (1, 0, 2)),
            )
        ]
    )


def last_shard(sz, place, top, bottom, w, q_gain, k_gain, state):
    far = sz.peers // 2
    heads = sz.cols // sz.head_dim

    def body(place_ref, top_ref, bottom_ref, w_ref, q_gain_ref, k_gain_ref, y_in, s1_in, s2_in, c_in, *refs):
        att_ref, gate_ref, mod_ref, whole_ref, y_ref, s1_ref, s2_ref, *rest = refs
        whole_ref[0 : sz.cut, :] = top_ref[...]
        whole_ref[sz.cut :, :] = bottom_ref[...]
        accumulate(
            sz,
            place_ref,
            [(far, whole_ref)],
            w_ref,
            mod_ref,
            (y_in, y_ref),
            (s1_in, s1_ref),
            (s2_in, s2_ref),
            c_in,
        )
        gate_ref[0] = whole_ref[sz.gate_at : sz.gate_at + sz.mod_rows, :]
        attend(sz, q_gain_ref, k_gain_ref, y_ref, s1_ref, s2_ref, *rest, att_ref)

    operands = [place, top, bottom, w, q_gain, k_gain, *state]
    bf16, f32 = jnp.bfloat16, jnp.float32
    return pl.pallas_call(
        body,
        out_shape=[
            jax.ShapeDtypeStruct((sz.slots * sz.image_len, sz.cols), bf16),
            jax.ShapeDtypeStruct((1, sz.mod_rows, sz.width), bf16),
        ],
        in_specs=[SM] + [VM] * (len(operands) - 1),
        out_specs=[VM] * 2,
        scratch_shapes=[
            pltpu.VMEM((sz.work_rows, sz.width), bf16),
            pltpu.VMEM((sz.payload, sz.width), bf16),
            pltpu.VMEM((3, sz.work_rows, sz.cols), f32),
            pltpu.VMEM((sz.token_rows, 128), f32),
            pltpu.VMEM((sz.token_rows, 128), f32),
            pltpu.VMEM((sz.token_rows, 128), f32),
            pltpu.VMEM((sz.token_rows, 128), f32),
            pltpu.VMEM((sz.slots, sz.image_len, sz.cols), bf16),
            pltpu.VMEM((sz.slots, heads * sz.seq, sz.cols), bf16),
            pltpu.VMEM((sz.slots, heads * sz.seq, sz.cols), bf16),
            pltpu.VMEM((heads * sz.seq, sz.cols), bf16),
            pltpu.VMEM((sz.slots, sz.image_len, heads * sz.seq), f32),
        ],
        compiler_params=PARAMS,
        cost_estimate=pl.CostEstimate(flops=6_000_000_000, transcendentals=0, bytes_accessed=1_000_000),
        name="attend",
    )(*operands)


def output_parts(sz, place, offsets, gates, w_out, coef, att, name):
    count = len(offsets)

    def body(place_ref, coef_ref, w_out_ref, att_ref, *refs):
        rows = [ref[at].astype(jnp.float32) for ref, (_, at) in zip(refs[:count], gates)]
        project_out(sz, place_ref, offsets, rows, w_out_ref, coef_ref, att_ref, refs[count:])

    return pl.pallas_call(
        body,
        out_shape=[jax.ShapeDtypeStruct((sz.image_rows, sz.width), jnp.bfloat16)] * count,
        in_specs=[SM, SM] + [VM] * (2 + count),
        out_specs=[VM] * count,
        compiler_params=PARAMS,
        cost_estimate=pl.CostEstimate(flops=300_000_000 * count, transcendentals=0, bytes_accessed=1_000_000),
        name=name,
    )(place, coef, w_out, att, *[array for array, _ in gates])


def on_device(
    image_latents,
    text_states,
    modulation,
    w_qkv,
    w_out,
    q_gain,
    k_gain,
    branch_count,
    branch_sign,
    guide_weight,
):
    images, image_len, width = image_latents.shape
    slots, text_len, _ = text_states.shape
    peers = lax.axis_size("mp")
    sz = Sizes(images, image_len, slots, text_len, width, peers, q_gain.shape[0], w_out.shape[0])

    payload = pack(sz, image_latents, text_states, modulation)
    w = jnp.transpose(w_qkv, (1, 0, 2))
    place = (lax.axis_index("mp") + jnp.arange(peers, dtype=jnp.int32)) % peers

    is_live = (jnp.arange(sz.per_image, dtype=jnp.int32)[None, :] < branch_count[:, None]).reshape(-1)
    weights_live = jnp.where(is_live, guide_weight, 0).astype(jnp.float32)
    weight_total = jnp.sum(weights_live.reshape(images, sz.per_image), axis=1)
    coef = (2 * branch_sign - 1).astype(jnp.float32) * weights_live / jnp.repeat(weight_total, sz.per_image)
    coef_total = jnp.sum(coef.reshape(images, sz.per_image), axis=1)

    def shifted(x, by):
        return lax.ppermute(x, "mp", [(i, (i + by) % peers) for i in range(peers)])

    far = peers // 2
    ring = {0: payload}
    gates = {}
    below = above = payload
    state = None
    for step in range(1, far + 1):
        cut = sz.cut if step == far else 0
        below = shifted(below[:cut] if cut else below, 1)
        above = shifted(above[cut:] if cut else above, -1)
        offsets = [0] if step == 1 else [peers - step + 1, step - 1]
        state, rows = add_shards(
            sz, place, offsets, [ring[o] for o in offsets], w, state, f"project_{step}"
        )
        for at, offset in enumerate(offsets):
            gates[offset] = (rows, at)
        ring[peers - step], ring[step] = below, above
        below, above, state = lax.optimization_barrier((below, above, state))
    att, rows = last_shard(
        sz, place, below, above, w, q_gain.reshape(1, -1), k_gain.reshape(1, -1), state
    )
    gates[far] = (rows, 0)
    early = [far, far + 1, far - 1]
    late = [o for d in range(far - 2, 0, -1) for o in (d, peers - d)] + [0]
    parts = {}
    for name, group in (("parts_far", early), ("parts_near", late)):
        made = output_parts(sz, place, group, [gates[o] for o in group], w_out, coef, att, name)
        for offset, part in zip(group, made):
            parts[offset] = shifted(part, offset) if offset else part
    total = parts[0].astype(jnp.float32)
    for offset in early + late[:-1]:
        total = total + parts[offset].astype(jnp.float32)
    total = total.reshape(images, image_len, width)
    return (image_latents.astype(jnp.float32) * coef_total[:, None, None] + total).astype(jnp.bfloat16)


def solution(mesh):
    placed = (
        P("dp", None, "mp"),
        P("dp", None, "mp"),
        P("dp", None, "mp"),
        P(None, None, "mp"),
        P("mp", None),
        P(),
        P(),
        P("dp"),
        P("dp"),
        P("dp"),
    )
    return jax.shard_map(
        on_device, mesh=mesh, in_specs=placed, out_specs=P("dp", None, "mp"), check_vma=False
    )
```

```python
import jax
import jax.numpy as jnp
from jax import lax
from jax.experimental import pallas as pl
from jax.experimental.pallas import tpu as pltpu
from jax.sharding import PartitionSpec as P

epsilon = 1e-06
ROUND = 16


def up(rows):
    return -(-rows // ROUND) * ROUND


class Sizes:
    def __init__(self, images, image_len, slots, text_len, width, peers, head_dim, local_cols):
        self.images, self.image_len, self.slots, self.text_len = images, image_len, slots, text_len
        self.width, self.peers, self.head_dim, self.cols = width, peers, head_dim, local_cols
        self.per_image = slots // images
        self.seq = image_len + text_len
        self.image_rows = images * image_len
        self.token_rows = self.image_rows + slots * text_len
        self.mod_rows = up(slots + 1)
        self.shift_at = self.token_rows
        self.scale_at = self.shift_at + self.mod_rows
        self.gate_at = self.scale_at + self.mod_rows
        self.payload = self.gate_at + self.mod_rows
        self.cut = up(self.payload // 2)
        self.seq_rows = slots * self.seq
        self.work_rows = self.seq_rows + 2 * self.mod_rows


def accumulate(sz, place_ref, shards, w_ref, mod_ref, y_refs, s1_refs, s2_refs, c_ref):
    width, lanes = sz.width, 128
    (y_in, y_ref), (s1_in, s1_ref), (s2_in, s2_ref) = y_refs, s1_refs, s2_refs
    first = y_in is None
    s1 = None
    for at, (offset, payload) in enumerate(shards):
        tokens = payload[0 : sz.token_rows, :].astype(jnp.float32)
        if first and at == 0:
            center = jnp.broadcast_to(
                jnp.sum(tokens, axis=1, keepdims=True) * (1.0 / width), (sz.token_rows, lanes)
            )
            c_ref[...] = center
        elif at == 0:
            center = c_ref[...]
        tokens = tokens - jnp.concatenate([center] * (width // lanes), axis=1)
        squares = tokens * tokens
        for part in range(width // lanes):
            piece = tokens[:, part * lanes : (part + 1) * lanes]
            piece2 = squares[:, part * lanes : (part + 1) * lanes]
            if s1 is None:
                s1, s2 = piece, piece2
            else:
                s1, s2 = s1 + piece, s2 + piece2
        cols = slice(at * width, (at + 1) * width)
        scale = payload[sz.scale_at : sz.scale_at + sz.mod_rows, :].astype(jnp.float32)
        row = lax.broadcasted_iota(jnp.int32, scale.shape, 0)
        scale_one = jnp.where(row == sz.slots, 1.0, scale)
        for s in range(sz.slots):
            image = s // sz.per_image
            factor = 1.0 + scale[s : s + 1, :]
            picture = tokens[image * sz.image_len : (image + 1) * sz.image_len, :]
            text_at = sz.image_rows + s * sz.text_len
            text = tokens[text_at : text_at + sz.text_len, :]
            base = s * sz.seq
            mod_ref[base : base + sz.image_len, cols] = (picture * factor).astype(jnp.bfloat16)
            mod_ref[base + sz.image_len : base + sz.seq, cols] = (text * factor).astype(jnp.bfloat16)
        mod_ref[sz.seq_rows : sz.seq_rows + sz.mod_rows, cols] = scale_one.astype(jnp.bfloat16)
        mod_ref[sz.seq_rows + sz.mod_rows : sz.work_rows, cols] = payload[
            sz.shift_at : sz.shift_at + sz.mod_rows, :
        ]
    if first:
        s1_ref[...] = s1
        s2_ref[...] = s2
    else:
        s1_ref[...] = s1_in[...] + s1
        s2_ref[...] = s2_in[...] + s2
    for third in range(3):
        weights = jnp.concatenate(
            [
                w_ref[third, pl.ds(pl.multiple_of(place_ref[offset] * width, 128), width), :]
                for offset, _ in shards
            ],
            axis=0,
        )
        part = jnp.dot(
            mod_ref[:, 0 : len(shards) * width], weights, preferred_element_type=jnp.float32
        )
        if first:
            y_ref[third] = part
        else:
            y_ref[third] = y_in[third] + part


def rms_norm(values, gain):
    return values * lax.rsqrt(jnp.mean(values * values, axis=-1, keepdims=True) + epsilon) * gain


def attend(sz, q_gain_ref, k_gain_ref, y_ref, s1_ref, s2_ref, rb_ref, mb_ref, q_ref, k_ref, v_ref, sums_ref, scores_ref, att_ref):
    full = float(sz.width * sz.peers)
    dim, heads, seq, pic = sz.head_dim, sz.cols // sz.head_dim, sz.seq, sz.image_len
    mean = jnp.sum(s1_ref[...], axis=1, keepdims=True) * (1.0 / full)
    second = jnp.sum(s2_ref[...], axis=1, keepdims=True) * (1.0 / full)
    rstd = lax.rsqrt(jnp.maximum(second - mean * mean, 0.0) + epsilon)
    rb_ref[...] = jnp.broadcast_to(rstd, (sz.token_rows, 128))
    mb_ref[...] = jnp.broadcast_to(-mean * rstd, (sz.token_rows, 128))
    q_gain, k_gain = q_gain_ref[...], k_gain_ref[...]
    ones_at = sz.seq_rows + sz.slots
    zeros = jnp.zeros((seq, dim), jnp.bfloat16)
    ones = jnp.ones((seq, dim), jnp.bfloat16)
    for h in range(heads):
        for g in range(heads):
            sums_ref[h * seq : (h + 1) * seq, g * dim : (g + 1) * dim] = ones if g == h else zeros
    for s in range(sz.slots):
        image = s // sz.per_image
        text_at = sz.image_rows + s * sz.text_len
        scale_at, shift_at, base = sz.seq_rows + s, sz.seq_rows + sz.mod_rows + s, s * seq
        spans = [
            (0, pic, image * pic),
            (pic, seq, text_at),
        ]
        for h in range(heads):
            cs = slice(h * dim, (h + 1) * dim)
            for third in range(3):
                u = y_ref[third, scale_at : scale_at + 1, cs] + y_ref[third, ones_at : ones_at + 1, cs]
                v = y_ref[third, shift_at : shift_at + 1, cs]
                for lo, hi, at in spans[: 1 if third == 0 else 2]:
                    rows = slice(at, at + hi - lo)
                    value = y_ref[third, base + lo : base + hi, cs] * rb_ref[rows, :]
                    value = value + (mb_ref[rows, :] * u + v)
                    if third == 0:
                        q_ref[s, :, cs] = rms_norm(value, q_gain).astype(jnp.bfloat16)
                    else:
                        if third == 1:
                            value = rms_norm(value, k_gain)
                        out = k_ref if third == 1 else v_ref
                        out[s, h * seq + lo : h * seq + hi, cs] = value.astype(jnp.bfloat16)
            for g in range(heads):
                if g != h:
                    k_ref[s, h * seq : (h + 1) * seq, g * dim : (g + 1) * dim] = zeros
                    v_ref[s, h * seq : (h + 1) * seq, g * dim : (g + 1) * dim] = zeros
    for s in range(sz.slots):
        scores_ref[s] = lax.dot_general(
            q_ref[s], k_ref[s], (((1,), (1,)), ((), ())), preferred_element_type=jnp.float32
        ) * dim ** (-0.5)
    lane = lax.broadcasted_iota(jnp.int32, (pic, heads * seq), 1)
    sums_rhs = sums_ref[...]
    for s in range(sz.slots):
        scores = scores_ref[s]
        top = None
        for h in range(heads):
            mine = (lane >= h * seq) & (lane < (h + 1) * seq)
            peak = jnp.max(jnp.where(mine, scores, -jnp.inf), axis=1, keepdims=True)
            top = jnp.broadcast_to(peak, scores.shape) if top is None else jnp.where(mine, peak, top)
        e = jnp.exp(scores - top).astype(jnp.bfloat16)
        total = jnp.dot(e, sums_rhs, preferred_element_type=jnp.float32)
        mixed = jnp.dot(e, v_ref[s], preferred_element_type=jnp.float32)
        att_ref[s * pic : (s + 1) * pic, :] = (mixed / total).astype(jnp.bfloat16)


def project_out(sz, place_ref, offsets, gate_rows, w_out_ref, coef_ref, att_ref, out_refs):
    for offset, gates, out_ref in zip(offsets, gate_rows, out_refs):
        cols = pl.ds(pl.multiple_of(place_ref[offset] * sz.width, 128), sz.width)
        rows = jnp.dot(att_ref[...], w_out_ref[:, cols], preferred_element_type=jnp.float32)
        for image in range(sz.images):
            total = None
            for s in range(image * sz.per_image, (image + 1) * sz.per_image):
                term = rows[s * sz.image_len : (s + 1) * sz.image_len, :] * (
                    gates[s : s + 1, :] * coef_ref[s]
                )
                total = term if total is None else total + term
            out_ref[image * sz.image_len : (image + 1) * sz.image_len, :] = total.astype(jnp.bfloat16)


VM = pl.BlockSpec(memory_space=pltpu.VMEM)
SM = pl.BlockSpec(memory_space=pltpu.SMEM)
PARAMS = pltpu.CompilerParams(vmem_limit_bytes=40 * 1024 * 1024)


def state_shapes(sz):
    f32 = jnp.float32
    return [
        jax.ShapeDtypeStruct((3, sz.work_rows, sz.cols), f32),
        jax.ShapeDtypeStruct((sz.token_rows, 128), f32),
        jax.ShapeDtypeStruct((sz.token_rows, 128), f32),
        jax.ShapeDtypeStruct((sz.token_rows, 128), f32),
    ]


def add_shards(sz, place, offsets, payloads, w, state, name):
    first = state is None
    count = len(offsets)

    def body(place_ref, *refs):
        payload_refs, refs = refs[:count], refs[count:]
        w_ref, refs = refs[0], refs[1:]
        y_in, s1_in, s2_in, c_in = (None, None, None, refs[3]) if first else refs[:4]
        if not first:
            refs = refs[4:]
        y_ref, s1_ref, s2_ref, c_ref, gate_ref, mod_ref = refs
        accumulate(
            sz,
            place_ref,
            list(zip(offsets, payload_refs)),
            w_ref,
            mod_ref,
            (y_in, y_ref),
            (s1_in, s1_ref),
            (s2_in, s2_ref),
            c_ref if first else c_in,
        )
        if not first:
            c_ref[...] = c_in[...]
        for at, payload in enumerate(payload_refs):
            gate_ref[at] = payload[sz.gate_at : sz.gate_at + sz.mod_rows, :]

    operands = [place, *payloads, w] + ([] if first else list(state))
    aliases = {} if first else {2 + count + i: i for i in range(4)}
    gate_shape = jax.ShapeDtypeStruct((count, sz.mod_rows, sz.width), jnp.bfloat16)
    *state, gates = pl.pallas_call(
        body,
        out_shape=state_shapes(sz) + [gate_shape],
        in_specs=[SM] + [VM] * (len(operands) - 1),
        out_specs=[VM] * 5,
        scratch_shapes=[pltpu.VMEM((sz.work_rows, count * sz.width), jnp.bfloat16)],
        input_output_aliases=aliases,
        compiler_params=PARAMS,
        cost_estimate=pl.CostEstimate(
            flops=1_000_000_000 * count, transcendentals=0, bytes_accessed=1_000_000
        ),
        name=name,
    )(*operands)
    return state, gates


def pack(sz, image_latents, text_states, modulation):
    def body(image_hbm, text_hbm, mod_hbm, out_ref, mod_ref, sems):
        copies = [
            pltpu.make_async_copy(mod_hbm, mod_ref, sems.at[0]),
            pltpu.make_async_copy(image_hbm, out_ref.at[0 : sz.image_rows, :], sems.at[1]),
            pltpu.make_async_copy(
                text_hbm, out_ref.at[sz.image_rows : sz.token_rows, :], sems.at[2]
            ),
        ]
        for copy in copies:
            copy.start()
        copies[0].wait()
        for part in range(3):
            at = sz.shift_at + part * sz.mod_rows
            rows = jnp.concatenate(
                [mod_ref[part], jnp.zeros((sz.mod_rows - sz.slots, sz.width), jnp.bfloat16)], axis=0
            )
            out_ref[at : at + sz.mod_rows, :] = rows
        copies[1].wait()
        copies[2].wait()

    return pl.pallas_call(
        body,
        out_shape=jax.ShapeDtypeStruct((sz.payload, sz.width), jnp.bfloat16),
        in_specs=[pl.BlockSpec(memory_space=pltpu.HBM)] * 3,
        out_specs=VM,
        scratch_shapes=[
            pltpu.VMEM((3, sz.slots, sz.width), jnp.bfloat16),
            pltpu.SemaphoreType.DMA((3,)),
        ],
        compiler_params=PARAMS,
        name="pack",
    )(
        *[
            pltpu.with_memory_space_constraint(x, pltpu.HBM)
            for x in (
                image_latents.reshape(sz.image_rows, sz.width),
                text_states.reshape(sz.slots * sz.text_len, sz.width),
                jnp.transpose(modulation, (1, 0, 2)),
            )
        ]
    )


def last_shard(sz, place, top, bottom, w, w_out, coef, q_gain, k_gain, state, offsets, gates):
    far = sz.peers // 2
    heads = sz.cols // sz.head_dim
    count = len(offsets)

    def body(place_ref, coef_ref, top_ref, bottom_ref, w_ref, w_out_ref, q_gain_ref, k_gain_ref, y_in, s1_in, s2_in, c_in, *refs):
        gate_refs, refs = refs[: count - 1], refs[count - 1 :]
        out_refs, refs = refs[:count], refs[count:]
        att_ref, mod_ref, whole_ref, y_ref, s1_ref, s2_ref, *rest = refs
        whole_ref[0 : sz.cut, :] = top_ref[...]
        whole_ref[sz.cut :, :] = bottom_ref[...]
        accumulate(
            sz,
            place_ref,
            [(far, whole_ref)],
            w_ref,
            mod_ref,
            (y_in, y_ref),
            (s1_in, s1_ref),
            (s2_in, s2_ref),
            c_in,
        )
        attend(sz, q_gain_ref, k_gain_ref, y_ref, s1_ref, s2_ref, *rest, att_ref)
        rows = [whole_ref[sz.gate_at : sz.gate_at + sz.mod_rows, :].astype(jnp.float32)]
        rows += [ref[at].astype(jnp.float32) for ref, (_, at) in zip(gate_refs, gates)]
        project_out(sz, place_ref, offsets, rows, w_out_ref, coef_ref, att_ref, out_refs)

    operands = [place, coef, top, bottom, w, w_out, q_gain, k_gain, *state]
    operands += [array for array, _ in gates]
    bf16, f32 = jnp.bfloat16, jnp.float32
    return pl.pallas_call(
        body,
        out_shape=[jax.ShapeDtypeStruct((sz.image_rows, sz.width), bf16)] * count,
        in_specs=[SM, SM] + [VM] * (len(operands) - 2),
        out_specs=[VM] * count,
        scratch_shapes=[
            pltpu.VMEM((sz.slots * sz.image_len, sz.cols), bf16),
            pltpu.VMEM((sz.work_rows, sz.width), bf16),
            pltpu.VMEM((sz.payload, sz.width), bf16),
            pltpu.VMEM((3, sz.work_rows, sz.cols), f32),
            pltpu.VMEM((sz.token_rows, 128), f32),
            pltpu.VMEM((sz.token_rows, 128), f32),
            pltpu.VMEM((sz.token_rows, 128), f32),
            pltpu.VMEM((sz.token_rows, 128), f32),
            pltpu.VMEM((sz.slots, sz.image_len, sz.cols), bf16),
            pltpu.VMEM((sz.slots, heads * sz.seq, sz.cols), bf16),
            pltpu.VMEM((sz.slots, heads * sz.seq, sz.cols), bf16),
            pltpu.VMEM((heads * sz.seq, sz.cols), bf16),
            pltpu.VMEM((sz.slots, sz.image_len, heads * sz.seq), f32),
        ],
        compiler_params=PARAMS,
        cost_estimate=pl.CostEstimate(flops=6_000_000_000, transcendentals=0, bytes_accessed=1_000_000),
        name="attend",
    )(*operands)


def on_device(
    image_latents,
    text_states,
    modulation,
    w_qkv,
    w_out,
    q_gain,
    k_gain,
    branch_count,
    branch_sign,
    guide_weight,
):
    images, image_len, width = image_latents.shape
    slots, text_len, _ = text_states.shape
    peers = lax.axis_size("mp")
    sz = Sizes(images, image_len, slots, text_len, width, peers, q_gain.shape[0], w_out.shape[0])

    payload = pack(sz, image_latents, text_states, modulation)
    w = jnp.transpose(w_qkv, (1, 0, 2))
    place = (lax.axis_index("mp") + jnp.arange(peers, dtype=jnp.int32)) % peers

    is_live = (jnp.arange(sz.per_image, dtype=jnp.int32)[None, :] < branch_count[:, None]).reshape(-1)
    weights_live = jnp.where(is_live, guide_weight, 0).astype(jnp.float32)
    weight_total = jnp.sum(weights_live.reshape(images, sz.per_image), axis=1)
    coef = (2 * branch_sign - 1).astype(jnp.float32) * weights_live / jnp.repeat(weight_total, sz.per_image)
    coef_total = jnp.sum(coef.reshape(images, sz.per_image), axis=1)

    def shifted(x, by):
        return lax.ppermute(x, "mp", [(i, (i + by) % peers) for i in range(peers)])

    far = peers // 2
    ring = {0: payload}
    gates = {}
    below = above = payload
    state = None
    for step in range(1, far + 1):
        cut = sz.cut if step == far else 0
        below = shifted(below[:cut] if cut else below, 1)
        above = shifted(above[cut:] if cut else above, -1)
        offsets = [0] if step == 1 else [peers - step + 1, step - 1]
        state, rows = add_shards(
            sz, place, offsets, [ring[o] for o in offsets], w, state, f"project_{step}"
        )
        for at, offset in enumerate(offsets):
            gates[offset] = (rows, at)
        ring[peers - step], ring[step] = below, above
        below, above, state = lax.optimization_barrier((below, above, state))
    sends = [1, peers - 1, far] + [o for d in range(far - 1, 1, -1) for o in (peers - d, d)]
    offsets = [far, 0] + [o for o in sends if o != far]
    made = last_shard(
        sz,
        place,
        below,
        above,
        w,
        w_out,
        coef,
        q_gain.reshape(1, -1),
        k_gain.reshape(1, -1),
        state,
        offsets,
        [gates[o] for o in offsets[1:]],
    )
    parts = dict(zip(offsets, made))
    total = parts[0].astype(jnp.float32)
    for offset in sends:
        total = total + shifted(parts[offset], offset).astype(jnp.float32)
    total = total.reshape(images, image_len, width)
    return (image_latents.astype(jnp.float32) * coef_total[:, None, None] + total).astype(jnp.bfloat16)


def solution(mesh):
    placed = (
        P("dp", None, "mp"),
        P("dp", None, "mp"),
        P("dp", None, "mp"),
        P(None, None, "mp"),
        P("mp", None),
        P(),
        P(),
        P("dp"),
        P("dp"),
        P("dp"),
    )
    return jax.shard_map(
        on_device, mesh=mesh, in_specs=placed, out_specs=P("dp", None, "mp"), check_vma=False
    )
```

```python
import jax
import jax.numpy as jnp
from jax import lax
from jax.experimental import pallas as pl
from jax.experimental.pallas import tpu as pltpu
from jax.sharding import PartitionSpec as P

epsilon = 1e-06
ROUND = 16


def up(rows):
    return -(-rows // ROUND) * ROUND


class Sizes:
    def __init__(self, images, image_len, slots, text_len, width, peers, head_dim, local_cols):
        self.images, self.image_len, self.slots, self.text_len = images, image_len, slots, text_len
        self.width, self.peers, self.head_dim, self.cols = width, peers, head_dim, local_cols
        self.per_image = slots // images
        self.seq = image_len + text_len
        self.image_rows = images * image_len
        self.token_rows = self.image_rows + slots * text_len
        self.mod_rows = up(slots + 1)
        self.shift_at = self.token_rows
        self.scale_at = self.shift_at + self.mod_rows
        self.gate_at = self.scale_at + self.mod_rows
        self.payload = self.gate_at + self.mod_rows
        self.cut = up(self.payload // 2)
        self.seq_rows = slots * self.seq
        self.work_rows = self.seq_rows + 2 * self.mod_rows


def accumulate(sz, place_ref, shards, w_ref, mod_ref, y_refs, s1_refs, s2_refs, c_ref):
    width, lanes = sz.width, 128
    (y_in, y_ref), (s1_in, s1_ref), (s2_in, s2_ref) = y_refs, s1_refs, s2_refs
    first = y_in is None
    s1 = None
    for at, (offset, payload) in enumerate(shards):
        tokens = payload[0 : sz.token_rows, :].astype(jnp.float32)
        if first and at == 0:
            center = jnp.broadcast_to(
                jnp.sum(tokens, axis=1, keepdims=True) * (1.0 / width), (sz.token_rows, lanes)
            )
            c_ref[...] = center
        elif at == 0:
            center = c_ref[...]
        tokens = tokens - jnp.concatenate([center] * (width // lanes), axis=1)
        squares = tokens * tokens
        for part in range(width // lanes):
            piece = tokens[:, part * lanes : (part + 1) * lanes]
            piece2 = squares[:, part * lanes : (part + 1) * lanes]
            if s1 is None:
                s1, s2 = piece, piece2
            else:
                s1, s2 = s1 + piece, s2 + piece2
        cols = slice(at * width, (at + 1) * width)
        scale = payload[sz.scale_at : sz.scale_at + sz.mod_rows, :].astype(jnp.float32)
        row = lax.broadcasted_iota(jnp.int32, scale.shape, 0)
        scale_one = jnp.where(row == sz.slots, 1.0, scale)
        for s in range(sz.slots):
            image = s // sz.per_image
            factor = 1.0 + scale[s : s + 1, :]
            picture = tokens[image * sz.image_len : (image + 1) * sz.image_len, :]
            text_at = sz.image_rows + s * sz.text_len
            text = tokens[text_at : text_at + sz.text_len, :]
            base = s * sz.seq
            mod_ref[base : base + sz.image_len, cols] = (picture * factor).astype(jnp.bfloat16)
            mod_ref[base + sz.image_len : base + sz.seq, cols] = (text * factor).astype(jnp.bfloat16)
        mod_ref[sz.seq_rows : sz.seq_rows + sz.mod_rows, cols] = scale_one.astype(jnp.bfloat16)
        mod_ref[sz.seq_rows + sz.mod_rows : sz.work_rows, cols] = payload[
            sz.shift_at : sz.shift_at + sz.mod_rows, :
        ]
    if first:
        s1_ref[...] = s1
        s2_ref[...] = s2
    else:
        s1_ref[...] = s1_in[...] + s1
        s2_ref[...] = s2_in[...] + s2
    for third in range(3):
        weights = jnp.concatenate(
            [
                w_ref[third, pl.ds(pl.multiple_of(place_ref[offset] * width, 128), width), :]
                for offset, _ in shards
            ],
            axis=0,
        )
        part = jnp.dot(
            mod_ref[:, 0 : len(shards) * width], weights, preferred_element_type=jnp.float32
        )
        if first:
            y_ref[third] = part
        else:
            y_ref[third] = y_in[third] + part


def rms_norm(values, gain):
    return values * lax.rsqrt(jnp.mean(values * values, axis=-1, keepdims=True) + epsilon) * gain


def attend(sz, q_gain_ref, k_gain_ref, y_ref, s1_ref, s2_ref, rb_ref, mb_ref, q_ref, k_ref, v_ref, sums_ref, scores_ref, att_ref):
    full = float(sz.width * sz.peers)
    dim, heads, seq, pic = sz.head_dim, sz.cols // sz.head_dim, sz.seq, sz.image_len
    mean = jnp.sum(s1_ref[...], axis=1, keepdims=True) * (1.0 / full)
    second = jnp.sum(s2_ref[...], axis=1, keepdims=True) * (1.0 / full)
    rstd = lax.rsqrt(jnp.maximum(second - mean * mean, 0.0) + epsilon)
    rb_ref[...] = jnp.broadcast_to(rstd, (sz.token_rows, 128))
    mb_ref[...] = jnp.broadcast_to(-mean * rstd, (sz.token_rows, 128))
    q_gain, k_gain = q_gain_ref[...], k_gain_ref[...]
    ones_at = sz.seq_rows + sz.slots
    zeros = jnp.zeros((seq, dim), jnp.bfloat16)
    ones = jnp.ones((seq, dim), jnp.bfloat16)
    for h in range(heads):
        for g in range(heads):
            sums_ref[h * seq : (h + 1) * seq, g * dim : (g + 1) * dim] = ones if g == h else zeros
    for s in range(sz.slots):
        image = s // sz.per_image
        text_at = sz.image_rows + s * sz.text_len
        scale_at, shift_at, base = sz.seq_rows + s, sz.seq_rows + sz.mod_rows + s, s * seq
        spans = [
            (0, pic, image * pic),
            (pic, seq, text_at),
        ]
        for h in range(heads):
            cs = slice(h * dim, (h + 1) * dim)
            for third in range(3):
                u = y_ref[third, scale_at : scale_at + 1, cs] + y_ref[third, ones_at : ones_at + 1, cs]
                v = y_ref[third, shift_at : shift_at + 1, cs]
                for lo, hi, at in spans[: 1 if third == 0 else 2]:
                    rows = slice(at, at + hi - lo)
                    value = y_ref[third, base + lo : base + hi, cs] * rb_ref[rows, :]
                    value = value + (mb_ref[rows, :] * u + v)
                    if third == 0:
                        q_ref[s, :, cs] = rms_norm(value, q_gain).astype(jnp.bfloat16)
                    else:
                        if third == 1:
                            value = rms_norm(value, k_gain)
                        out = k_ref if third == 1 else v_ref
                        out[s, h * seq + lo : h * seq + hi, cs] = value.astype(jnp.bfloat16)
            for g in range(heads):
                if g != h:
                    k_ref[s, h * seq : (h + 1) * seq, g * dim : (g + 1) * dim] = zeros
                    v_ref[s, h * seq : (h + 1) * seq, g * dim : (g + 1) * dim] = zeros
    for s in range(sz.slots):
        scores_ref[s] = lax.dot_general(
            q_ref[s], k_ref[s], (((1,), (1,)), ((), ())), preferred_element_type=jnp.float32
        ) * dim ** (-0.5)
    lane = lax.broadcasted_iota(jnp.int32, (pic, heads * seq), 1)
    sums_rhs = sums_ref[...]
    for s in range(sz.slots):
        scores = scores_ref[s]
        top = None
        for h in range(heads):
            mine = (lane >= h * seq) & (lane < (h + 1) * seq)
            peak = jnp.max(jnp.where(mine, scores, -jnp.inf), axis=1, keepdims=True)
            top = jnp.broadcast_to(peak, scores.shape) if top is None else jnp.where(mine, peak, top)
        e = jnp.exp(scores - top).astype(jnp.bfloat16)
        total = jnp.dot(e, sums_rhs, preferred_element_type=jnp.float32)
        mixed = jnp.dot(e, v_ref[s], preferred_element_type=jnp.float32)
        att_ref[s * pic : (s + 1) * pic, :] = (mixed / total).astype(jnp.bfloat16)


def project_out(sz, place_ref, offsets, gate_rows, w_out_ref, coef_ref, att_ref, out_refs):
    for offset, gates, out_ref in zip(offsets, gate_rows, out_refs):
        cols = pl.ds(pl.multiple_of(place_ref[offset] * sz.width, 128), sz.width)
        rows = jnp.dot(att_ref[...], w_out_ref[:, cols], preferred_element_type=jnp.float32)
        for image in range(sz.images):
            total = None
            for s in range(image * sz.per_image, (image + 1) * sz.per_image):
                term = rows[s * sz.image_len : (s + 1) * sz.image_len, :] * (
                    gates[s : s + 1, :] * coef_ref[s]
                )
                total = term if total is None else total + term
            out_ref[image * sz.image_len : (image + 1) * sz.image_len, :] = total.astype(jnp.bfloat16)


VM = pl.BlockSpec(memory_space=pltpu.VMEM)
SM = pl.BlockSpec(memory_space=pltpu.SMEM)
PARAMS = pltpu.CompilerParams(vmem_limit_bytes=40 * 1024 * 1024)


def state_shapes(sz):
    f32 = jnp.float32
    return [
        jax.ShapeDtypeStruct((3, sz.work_rows, sz.cols), f32),
        jax.ShapeDtypeStruct((sz.token_rows, 128), f32),
        jax.ShapeDtypeStruct((sz.token_rows, 128), f32),
        jax.ShapeDtypeStruct((sz.token_rows, 128), f32),
    ]


def add_shards(sz, place, offsets, payloads, w, state, name):
    first = state is None
    count = len(offsets)

    def body(place_ref, *refs):
        payload_refs, refs = refs[:count], refs[count:]
        w_ref, refs = refs[0], refs[1:]
        y_in, s1_in, s2_in, c_in = (None, None, None, refs[3]) if first else refs[:4]
        if not first:
            refs = refs[4:]
        y_ref, s1_ref, s2_ref, c_ref, gate_ref, mod_ref = refs
        accumulate(
            sz,
            place_ref,
            list(zip(offsets, payload_refs)),
            w_ref,
            mod_ref,
            (y_in, y_ref),
            (s1_in, s1_ref),
            (s2_in, s2_ref),
            c_ref if first else c_in,
        )
        if not first:
            c_ref[...] = c_in[...]
        for at, payload in enumerate(payload_refs):
            gate_ref[at] = payload[sz.gate_at : sz.gate_at + sz.mod_rows, :]

    operands = [place, *payloads, w] + ([] if first else list(state))
    aliases = {} if first else {2 + count + i: i for i in range(4)}
    gate_shape = jax.ShapeDtypeStruct((count, sz.mod_rows, sz.width), jnp.bfloat16)
    *state, gates = pl.pallas_call(
        body,
        out_shape=state_shapes(sz) + [gate_shape],
        in_specs=[SM] + [VM] * (len(operands) - 1),
        out_specs=[VM] * 5,
        scratch_shapes=[pltpu.VMEM((sz.work_rows, count * sz.width), jnp.bfloat16)],
        input_output_aliases=aliases,
        compiler_params=PARAMS,
        cost_estimate=pl.CostEstimate(
            flops=1_000_000_000 * count, transcendentals=0, bytes_accessed=1_000_000
        ),
        name=name,
    )(*operands)
    return state, gates


def pack(sz, image_latents, text_states, modulation):
    def body(image_hbm, text_hbm, mod_hbm, out_ref, mod_ref, sems):
        copies = [
            pltpu.make_async_copy(mod_hbm, mod_ref, sems.at[0]),
            pltpu.make_async_copy(image_hbm, out_ref.at[0 : sz.image_rows, :], sems.at[1]),
            pltpu.make_async_copy(
                text_hbm, out_ref.at[sz.image_rows : sz.token_rows, :], sems.at[2]
            ),
        ]
        for copy in copies:
            copy.start()
        copies[0].wait()
        for part in range(3):
            at = sz.shift_at + part * sz.mod_rows
            rows = jnp.concatenate(
                [mod_ref[part], jnp.zeros((sz.mod_rows - sz.slots, sz.width), jnp.bfloat16)], axis=0
            )
            out_ref[at : at + sz.mod_rows, :] = rows
        copies[1].wait()
        copies[2].wait()

    return pl.pallas_call(
        body,
        out_shape=jax.ShapeDtypeStruct((sz.payload, sz.width), jnp.bfloat16),
        in_specs=[pl.BlockSpec(memory_space=pltpu.HBM)] * 3,
        out_specs=VM,
        scratch_shapes=[
            pltpu.VMEM((3, sz.slots, sz.width), jnp.bfloat16),
            pltpu.SemaphoreType.DMA((3,)),
        ],
        compiler_params=PARAMS,
        name="pack",
    )(
        *[
            pltpu.with_memory_space_constraint(x, pltpu.HBM)
            for x in (
                image_latents.reshape(sz.image_rows, sz.width),
                text_states.reshape(sz.slots * sz.text_len, sz.width),
                jnp.transpose(modulation, (1, 0, 2)),
            )
        ]
    )


def last_shard(sz, place, top, bottom, w, q_gain, k_gain, state):
    far = sz.peers // 2
    heads = sz.cols // sz.head_dim

    def body(place_ref, top_ref, bottom_ref, w_ref, q_gain_ref, k_gain_ref, y_in, s1_in, s2_in, c_in, *refs):
        att_ref, gate_ref, mod_ref, whole_ref, y_ref, s1_ref, s2_ref, *rest = refs
        whole_ref[0 : sz.cut, :] = top_ref[...]
        whole_ref[sz.cut :, :] = bottom_ref[...]
        accumulate(
            sz,
            place_ref,
            [(far, whole_ref)],
            w_ref,
            mod_ref,
            (y_in, y_ref),
            (s1_in, s1_ref),
            (s2_in, s2_ref),
            c_in,
        )
        gate_ref[0] = whole_ref[sz.gate_at : sz.gate_at + sz.mod_rows, :]
        attend(sz, q_gain_ref, k_gain_ref, y_ref, s1_ref, s2_ref, *rest, att_ref)

    operands = [place, top, bottom, w, q_gain, k_gain, *state]
    bf16, f32 = jnp.bfloat16, jnp.float32
    return pl.pallas_call(
        body,
        out_shape=[
            jax.ShapeDtypeStruct((sz.slots * sz.image_len, sz.cols), bf16),
            jax.ShapeDtypeStruct((1, sz.mod_rows, sz.width), bf16),
        ],
        in_specs=[SM] + [VM] * (len(operands) - 1),
        out_specs=[VM] * 2,
        scratch_shapes=[
            pltpu.VMEM((sz.work_rows, sz.width), bf16),
            pltpu.VMEM((sz.payload, sz.width), bf16),
            pltpu.VMEM((3, sz.work_rows, sz.cols), f32),
            pltpu.VMEM((sz.token_rows, 128), f32),
            pltpu.VMEM((sz.token_rows, 128), f32),
            pltpu.VMEM((sz.token_rows, 128), f32),
            pltpu.VMEM((sz.token_rows, 128), f32),
            pltpu.VMEM((sz.slots, sz.image_len, sz.cols), bf16),
            pltpu.VMEM((sz.slots, heads * sz.seq, sz.cols), bf16),
            pltpu.VMEM((sz.slots, heads * sz.seq, sz.cols), bf16),
            pltpu.VMEM((heads * sz.seq, sz.cols), bf16),
            pltpu.VMEM((sz.slots, sz.image_len, heads * sz.seq), f32),
        ],
        compiler_params=PARAMS,
        cost_estimate=pl.CostEstimate(flops=6_000_000_000, transcendentals=0, bytes_accessed=1_000_000),
        name="attend",
    )(*operands)


def output_parts(sz, place, offsets, gates, w_out, coef, att, name):
    count = len(offsets)

    def body(place_ref, coef_ref, w_out_ref, att_ref, *refs):
        rows = [ref[at].astype(jnp.float32) for ref, (_, at) in zip(refs[:count], gates)]
        project_out(sz, place_ref, offsets, rows, w_out_ref, coef_ref, att_ref, refs[count:])

    return pl.pallas_call(
        body,
        out_shape=[jax.ShapeDtypeStruct((sz.image_rows, sz.width), jnp.bfloat16)] * count,
        in_specs=[SM, SM] + [VM] * (2 + count),
        out_specs=[VM] * count,
        compiler_params=PARAMS,
        cost_estimate=pl.CostEstimate(flops=300_000_000 * count, transcendentals=0, bytes_accessed=1_000_000),
        name=name,
    )(place, coef, w_out, att, *[array for array, _ in gates])


def on_device(
    image_latents,
    text_states,
    modulation,
    w_qkv,
    w_out,
    q_gain,
    k_gain,
    branch_count,
    branch_sign,
    guide_weight,
):
    images, image_len, width = image_latents.shape
    slots, text_len, _ = text_states.shape
    peers = lax.axis_size("mp")
    sz = Sizes(images, image_len, slots, text_len, width, peers, q_gain.shape[0], w_out.shape[0])

    payload = pack(sz, image_latents, text_states, modulation)
    w = jnp.transpose(w_qkv, (1, 0, 2))
    place = (lax.axis_index("mp") + jnp.arange(peers, dtype=jnp.int32)) % peers

    is_live = (jnp.arange(sz.per_image, dtype=jnp.int32)[None, :] < branch_count[:, None]).reshape(-1)
    weights_live = jnp.where(is_live, guide_weight, 0).astype(jnp.float32)
    weight_total = jnp.sum(weights_live.reshape(images, sz.per_image), axis=1)
    coef = (2 * branch_sign - 1).astype(jnp.float32) * weights_live / jnp.repeat(weight_total, sz.per_image)
    coef_total = jnp.sum(coef.reshape(images, sz.per_image), axis=1)

    def shifted(x, by):
        return lax.ppermute(x, "mp", [(i, (i + by) % peers) for i in range(peers)])

    far = peers // 2
    ring = {0: payload}
    gates = {}
    below = above = payload
    state = None
    for step in range(1, far + 1):
        cut = sz.cut if step == far else 0
        above = shifted(above[cut:] if cut else above, -1)
        below = shifted(below[:cut] if cut else below, 1)
        offsets = [0] if step == 1 else [peers - step + 1, step - 1]
        state, rows = add_shards(
            sz, place, offsets, [ring[o] for o in offsets], w, state, f"project_{step}"
        )
        for at, offset in enumerate(offsets):
            gates[offset] = (rows, at)
        ring[peers - step], ring[step] = below, above
        below, above, state = lax.optimization_barrier((below, above, state))
    att, rows = last_shard(
        sz, place, below, above, w, q_gain.reshape(1, -1), k_gain.reshape(1, -1), state
    )
    gates[far] = (rows, 0)
    early = [far - 1, far, far + 1]
    late = [o for d in range(far - 2, 0, -1) for o in (d, peers - d)] + [0]
    parts = {}
    for name, group in (("parts_far", early), ("parts_near", late)):
        made = output_parts(sz, place, group, [gates[o] for o in group], w_out, coef, att, name)
        for offset, part in zip(group, made):
            parts[offset] = shifted(part, offset) if offset else part
    total = parts[0].astype(jnp.float32)
    for offset in early + late[:-1]:
        total = total + parts[offset].astype(jnp.float32)
    total = total.reshape(images, image_len, width)
    return (image_latents.astype(jnp.float32) * coef_total[:, None, None] + total).astype(jnp.bfloat16)


def solution(mesh):
    placed = (
        P("dp", None, "mp"),
        P("dp", None, "mp"),
        P("dp", None, "mp"),
        P(None, None, "mp"),
        P("mp", None),
        P(),
        P(),
        P("dp"),
        P("dp"),
        P("dp"),
    )
    return jax.shard_map(
        on_device, mesh=mesh, in_specs=placed, out_specs=P("dp", None, "mp"), check_vma=False
    )
```

```python
import jax
import jax.numpy as jnp
from jax import lax
from jax.experimental import pallas as pl
from jax.experimental.pallas import tpu as pltpu
from jax.sharding import PartitionSpec as P

epsilon = 1e-06
ROUND = 16


def up(rows):
    return -(-rows // ROUND) * ROUND


class Sizes:
    def __init__(self, images, image_len, slots, text_len, width, peers, head_dim, local_cols):
        self.images, self.image_len, self.slots, self.text_len = images, image_len, slots, text_len
        self.width, self.peers, self.head_dim, self.cols = width, peers, head_dim, local_cols
        self.per_image = slots // images
        self.seq = image_len + text_len
        self.image_rows = images * image_len
        self.token_rows = self.image_rows + slots * text_len
        self.mod_rows = up(slots + 1)
        self.shift_at = self.token_rows
        self.scale_at = self.shift_at + self.mod_rows
        self.gate_at = self.scale_at + self.mod_rows
        self.payload = self.gate_at + self.mod_rows
        self.cut = up(self.payload // 2)
        self.seq_rows = slots * self.seq
        self.work_rows = self.seq_rows + 2 * self.mod_rows


def accumulate(sz, place_ref, shards, w_ref, mod_ref, y_refs, s1_refs, s2_refs, c_ref):
    width, lanes = sz.width, 128
    (y_in, y_ref), (s1_in, s1_ref), (s2_in, s2_ref) = y_refs, s1_refs, s2_refs
    first = y_in is None
    s1 = None
    for at, (offset, payload) in enumerate(shards):
        tokens = payload[0 : sz.token_rows, :].astype(jnp.float32)
        if first and at == 0:
            center = jnp.broadcast_to(
                jnp.sum(tokens, axis=1, keepdims=True) * (1.0 / width), (sz.token_rows, lanes)
            )
            c_ref[...] = center
        elif at == 0:
            center = c_ref[...]
        tokens = tokens - jnp.concatenate([center] * (width // lanes), axis=1)
        squares = tokens * tokens
        for part in range(width // lanes):
            piece = tokens[:, part * lanes : (part + 1) * lanes]
            piece2 = squares[:, part * lanes : (part + 1) * lanes]
            if s1 is None:
                s1, s2 = piece, piece2
            else:
                s1, s2 = s1 + piece, s2 + piece2
        cols = slice(at * width, (at + 1) * width)
        scale = payload[sz.scale_at : sz.scale_at + sz.mod_rows, :].astype(jnp.float32)
        row = lax.broadcasted_iota(jnp.int32, scale.shape, 0)
        scale_one = jnp.where(row == sz.slots, 1.0, scale)
        for s in range(sz.slots):
            image = s // sz.per_image
            factor = 1.0 + scale[s : s + 1, :]
            picture = tokens[image * sz.image_len : (image + 1) * sz.image_len, :]
            text_at = sz.image_rows + s * sz.text_len
            text = tokens[text_at : text_at + sz.text_len, :]
            base = s * sz.seq
            mod_ref[base : base + sz.image_len, cols] = (picture * factor).astype(jnp.bfloat16)
            mod_ref[base + sz.image_len : base + sz.seq, cols] = (text * factor).astype(jnp.bfloat16)
        mod_ref[sz.seq_rows : sz.seq_rows + sz.mod_rows, cols] = scale_one.astype(jnp.bfloat16)
        mod_ref[sz.seq_rows + sz.mod_rows : sz.work_rows, cols] = payload[
            sz.shift_at : sz.shift_at + sz.mod_rows, :
        ]
    if first:
        s1_ref[...] = s1
        s2_ref[...] = s2
    else:
        s1_ref[...] = s1_in[...] + s1
        s2_ref[...] = s2_in[...] + s2
    for third in range(3):
        weights = jnp.concatenate(
            [
                w_ref[third, pl.ds(pl.multiple_of(place_ref[offset] * width, 128), width), :]
                for offset, _ in shards
            ],
            axis=0,
        )
        part = jnp.dot(
            mod_ref[:, 0 : len(shards) * width], weights, preferred_element_type=jnp.float32
        )
        if first:
            y_ref[third] = part
        else:
            y_ref[third] = y_in[third] + part


def rms_norm(values, gain):
    return values * lax.rsqrt(jnp.mean(values * values, axis=-1, keepdims=True) + epsilon) * gain


def attend(sz, q_gain_ref, k_gain_ref, y_ref, s1_ref, s2_ref, rb_ref, mb_ref, q_ref, k_ref, v_ref, sums_ref, scores_ref, att_ref):
    full = float(sz.width * sz.peers)
    dim, heads, seq, pic = sz.head_dim, sz.cols // sz.head_dim, sz.seq, sz.image_len
    mean = jnp.sum(s1_ref[...], axis=1, keepdims=True) * (1.0 / full)
    second = jnp.sum(s2_ref[...], axis=1, keepdims=True) * (1.0 / full)
    rstd = lax.rsqrt(jnp.maximum(second - mean * mean, 0.0) + epsilon)
    rb_ref[...] = jnp.broadcast_to(rstd, (sz.token_rows, 128))
    mb_ref[...] = jnp.broadcast_to(-mean * rstd, (sz.token_rows, 128))
    q_gain, k_gain = q_gain_ref[...], k_gain_ref[...]
    ones_at = sz.seq_rows + sz.slots
    zeros = jnp.zeros((seq, dim), jnp.bfloat16)
    ones = jnp.ones((seq, dim), jnp.bfloat16)
    for h in range(heads):
        for g in range(heads):
            sums_ref[h * seq : (h + 1) * seq, g * dim : (g + 1) * dim] = ones if g == h else zeros
    for s in range(sz.slots):
        image = s // sz.per_image
        text_at = sz.image_rows + s * sz.text_len
        scale_at, shift_at, base = sz.seq_rows + s, sz.seq_rows + sz.mod_rows + s, s * seq
        spans = []
        for lo, hi, at in ((0, pic, image * pic), (pic, seq, text_at)):
            rows = slice(at, at + hi - lo)
            spans.append((lo, hi, rb_ref[rows, :], mb_ref[rows, :]))
        for h in range(heads):
            cs = slice(h * dim, (h + 1) * dim)
            for third in range(3):
                u = y_ref[third, scale_at : scale_at + 1, cs] + y_ref[third, ones_at : ones_at + 1, cs]
                v = y_ref[third, shift_at : shift_at + 1, cs]
                for lo, hi, r, m in spans[: 1 if third == 0 else 2]:
                    value = y_ref[third, base + lo : base + hi, cs] * r + (m * u + v)
                    if third == 0:
                        q_ref[s, :, cs] = rms_norm(value, q_gain).astype(jnp.bfloat16)
                    else:
                        if third == 1:
                            value = rms_norm(value, k_gain)
                        out = k_ref if third == 1 else v_ref
                        out[s, h * seq + lo : h * seq + hi, cs] = value.astype(jnp.bfloat16)
            for g in range(heads):
                if g != h:
                    k_ref[s, h * seq : (h + 1) * seq, g * dim : (g + 1) * dim] = zeros
                    v_ref[s, h * seq : (h + 1) * seq, g * dim : (g + 1) * dim] = zeros
    for s in range(sz.slots):
        scores_ref[s] = lax.dot_general(
            q_ref[s], k_ref[s], (((1,), (1,)), ((), ())), preferred_element_type=jnp.float32
        ) * dim ** (-0.5)
    lane = lax.broadcasted_iota(jnp.int32, (pic, heads * seq), 1)
    sums_rhs = sums_ref[...]
    for s in range(sz.slots):
        scores = scores_ref[s]
        top = None
        for h in range(heads):
            mine = (lane >= h * seq) & (lane < (h + 1) * seq)
            peak = jnp.max(jnp.where(mine, scores, -jnp.inf), axis=1, keepdims=True)
            top = jnp.broadcast_to(peak, scores.shape) if top is None else jnp.where(mine, peak, top)
        e = jnp.exp(scores - top).astype(jnp.bfloat16)
        total = jnp.dot(e, sums_rhs, preferred_element_type=jnp.float32)
        mixed = jnp.dot(e, v_ref[s], preferred_element_type=jnp.float32)
        att_ref[s * pic : (s + 1) * pic, :] = (mixed / total).astype(jnp.bfloat16)


def project_out(sz, place_ref, offsets, gate_rows, w_out_ref, coef_ref, att_ref, out_refs):
    for offset, gates, out_ref in zip(offsets, gate_rows, out_refs):
        cols = pl.ds(pl.multiple_of(place_ref[offset] * sz.width, 128), sz.width)
        rows = jnp.dot(att_ref[...], w_out_ref[:, cols], preferred_element_type=jnp.float32)
        for image in range(sz.images):
            total = None
            for s in range(image * sz.per_image, (image + 1) * sz.per_image):
                term = rows[s * sz.image_len : (s + 1) * sz.image_len, :] * (
                    gates[s : s + 1, :] * coef_ref[s]
                )
                total = term if total is None else total + term
            out_ref[image * sz.image_len : (image + 1) * sz.image_len, :] = total.astype(jnp.bfloat16)


VM = pl.BlockSpec(memory_space=pltpu.VMEM)
SM = pl.BlockSpec(memory_space=pltpu.SMEM)
PARAMS = pltpu.CompilerParams(vmem_limit_bytes=40 * 1024 * 1024)


def state_shapes(sz):
    f32 = jnp.float32
    return [
        jax.ShapeDtypeStruct((3, sz.work_rows, sz.cols), f32),
        jax.ShapeDtypeStruct((sz.token_rows, 128), f32),
        jax.ShapeDtypeStruct((sz.token_rows, 128), f32),
        jax.ShapeDtypeStruct((sz.token_rows, 128), f32),
    ]


def add_shards(sz, place, offsets, payloads, w, state, name):
    first = state is None
    count = len(offsets)

    def body(place_ref, *refs):
        payload_refs, refs = refs[:count], refs[count:]
        w_ref, refs = refs[0], refs[1:]
        y_in, s1_in, s2_in, c_in = (None, None, None, refs[3]) if first else refs[:4]
        if not first:
            refs = refs[4:]
        y_ref, s1_ref, s2_ref, c_ref, gate_ref, mod_ref = refs
        accumulate(
            sz,
            place_ref,
            list(zip(offsets, payload_refs)),
            w_ref,
            mod_ref,
            (y_in, y_ref),
            (s1_in, s1_ref),
            (s2_in, s2_ref),
            c_ref if first else c_in,
        )
        if not first:
            c_ref[...] = c_in[...]
        for at, payload in enumerate(payload_refs):
            gate_ref[at] = payload[sz.gate_at : sz.gate_at + sz.mod_rows, :]

    operands = [place, *payloads, w] + ([] if first else list(state))
    aliases = {} if first else {2 + count + i: i for i in range(4)}
    gate_shape = jax.ShapeDtypeStruct((count, sz.mod_rows, sz.width), jnp.bfloat16)
    *state, gates = pl.pallas_call(
        body,
        out_shape=state_shapes(sz) + [gate_shape],
        in_specs=[SM] + [VM] * (len(operands) - 1),
        out_specs=[VM] * 5,
        scratch_shapes=[pltpu.VMEM((sz.work_rows, count * sz.width), jnp.bfloat16)],
        input_output_aliases=aliases,
        compiler_params=PARAMS,
        cost_estimate=pl.CostEstimate(
            flops=1_000_000_000 * count, transcendentals=0, bytes_accessed=1_000_000
        ),
        name=name,
    )(*operands)
    return state, gates


def pack(sz, image_latents, text_states, modulation):
    def body(image_hbm, text_hbm, mod_hbm, out_ref, mod_ref, sems):
        copies = [
            pltpu.make_async_copy(mod_hbm, mod_ref, sems.at[0]),
            pltpu.make_async_copy(image_hbm, out_ref.at[0 : sz.image_rows, :], sems.at[1]),
            pltpu.make_async_copy(
                text_hbm, out_ref.at[sz.image_rows : sz.token_rows, :], sems.at[2]
            ),
        ]
        for copy in copies:
            copy.start()
        copies[0].wait()
        for part in range(3):
            at = sz.shift_at + part * sz.mod_rows
            rows = jnp.concatenate(
                [mod_ref[part], jnp.zeros((sz.mod_rows - sz.slots, sz.width), jnp.bfloat16)], axis=0
            )
            out_ref[at : at + sz.mod_rows, :] = rows
        copies[1].wait()
        copies[2].wait()

    return pl.pallas_call(
        body,
        out_shape=jax.ShapeDtypeStruct((sz.payload, sz.width), jnp.bfloat16),
        in_specs=[pl.BlockSpec(memory_space=pltpu.HBM)] * 3,
        out_specs=VM,
        scratch_shapes=[
            pltpu.VMEM((3, sz.slots, sz.width), jnp.bfloat16),
            pltpu.SemaphoreType.DMA((3,)),
        ],
        compiler_params=PARAMS,
        name="pack",
    )(
        *[
            pltpu.with_memory_space_constraint(x, pltpu.HBM)
            for x in (
                image_latents.reshape(sz.image_rows, sz.width),
                text_states.reshape(sz.slots * sz.text_len, sz.width),
                jnp.transpose(modulation, (1, 0, 2)),
            )
        ]
    )


def last_shard(sz, place, top, bottom, w, q_gain, k_gain, state):
    far = sz.peers // 2
    heads = sz.cols // sz.head_dim

    def body(place_ref, top_ref, bottom_ref, w_ref, q_gain_ref, k_gain_ref, y_in, s1_in, s2_in, c_in, *refs):
        att_ref, gate_ref, mod_ref, whole_ref, y_ref, s1_ref, s2_ref, *rest = refs
        whole_ref[0 : sz.cut, :] = top_ref[...]
        whole_ref[sz.cut :, :] = bottom_ref[...]
        accumulate(
            sz,
            place_ref,
            [(far, whole_ref)],
            w_ref,
            mod_ref,
            (y_in, y_ref),
            (s1_in, s1_ref),
            (s2_in, s2_ref),
            c_in,
        )
        gate_ref[0] = whole_ref[sz.gate_at : sz.gate_at + sz.mod_rows, :]
        attend(sz, q_gain_ref, k_gain_ref, y_ref, s1_ref, s2_ref, *rest, att_ref)

    operands = [place, top, bottom, w, q_gain, k_gain, *state]
    bf16, f32 = jnp.bfloat16, jnp.float32
    return pl.pallas_call(
        body,
        out_shape=[
            jax.ShapeDtypeStruct((sz.slots * sz.image_len, sz.cols), bf16),
            jax.ShapeDtypeStruct((1, sz.mod_rows, sz.width), bf16),
        ],
        in_specs=[SM] + [VM] * (len(operands) - 1),
        out_specs=[VM] * 2,
        scratch_shapes=[
            pltpu.VMEM((sz.work_rows, sz.width), bf16),
            pltpu.VMEM((sz.payload, sz.width), bf16),
            pltpu.VMEM((3, sz.work_rows, sz.cols), f32),
            pltpu.VMEM((sz.token_rows, 128), f32),
            pltpu.VMEM((sz.token_rows, 128), f32),
            pltpu.VMEM((sz.token_rows, 128), f32),
            pltpu.VMEM((sz.token_rows, 128), f32),
            pltpu.VMEM((sz.slots, sz.image_len, sz.cols), bf16),
            pltpu.VMEM((sz.slots, heads * sz.seq, sz.cols), bf16),
            pltpu.VMEM((sz.slots, heads * sz.seq, sz.cols), bf16),
            pltpu.VMEM((heads * sz.seq, sz.cols), bf16),
            pltpu.VMEM((sz.slots, sz.image_len, heads * sz.seq), f32),
        ],
        compiler_params=PARAMS,
        cost_estimate=pl.CostEstimate(flops=6_000_000_000, transcendentals=0, bytes_accessed=1_000_000),
        name="attend",
    )(*operands)


def output_parts(sz, place, offsets, gates, w_out, coef, att, name):
    count = len(offsets)

    def body(place_ref, coef_ref, w_out_ref, att_ref, *refs):
        rows = [ref[at].astype(jnp.float32) for ref, (_, at) in zip(refs[:count], gates)]
        project_out(sz, place_ref, offsets, rows, w_out_ref, coef_ref, att_ref, refs[count:])

    return pl.pallas_call(
        body,
        out_shape=[jax.ShapeDtypeStruct((sz.image_rows, sz.width), jnp.bfloat16)] * count,
        in_specs=[SM, SM] + [VM] * (2 + count),
        out_specs=[VM] * count,
        compiler_params=PARAMS,
        cost_estimate=pl.CostEstimate(flops=300_000_000 * count, transcendentals=0, bytes_accessed=1_000_000),
        name=name,
    )(place, coef, w_out, att, *[array for array, _ in gates])


def on_device(
    image_latents,
    text_states,
    modulation,
    w_qkv,
    w_out,
    q_gain,
    k_gain,
    branch_count,
    branch_sign,
    guide_weight,
):
    images, image_len, width = image_latents.shape
    slots, text_len, _ = text_states.shape
    peers = lax.axis_size("mp")
    sz = Sizes(images, image_len, slots, text_len, width, peers, q_gain.shape[0], w_out.shape[0])

    payload = pack(sz, image_latents, text_states, modulation)
    w = jnp.transpose(w_qkv, (1, 0, 2))
    place = (lax.axis_index("mp") + jnp.arange(peers, dtype=jnp.int32)) % peers

    is_live = (jnp.arange(sz.per_image, dtype=jnp.int32)[None, :] < branch_count[:, None]).reshape(-1)
    weights_live = jnp.where(is_live, guide_weight, 0).astype(jnp.float32)
    weight_total = jnp.sum(weights_live.reshape(images, sz.per_image), axis=1)
    coef = (2 * branch_sign - 1).astype(jnp.float32) * weights_live / jnp.repeat(weight_total, sz.per_image)
    coef_total = jnp.sum(coef.reshape(images, sz.per_image), axis=1)

    def shifted(x, by):
        return lax.ppermute(x, "mp", [(i, (i + by) % peers) for i in range(peers)])

    far = peers // 2
    ring = {0: payload}
    gates = {}
    below = above = payload
    state = None
    for step in range(1, far + 1):
        cut = sz.cut if step == far else 0
        above = shifted(above[cut:] if cut else above, -1)
        below = shifted(below[:cut] if cut else below, 1)
        offsets = [0] if step == 1 else [peers - step + 1, step - 1]
        state, rows = add_shards(
            sz, place, offsets, [ring[o] for o in offsets], w, state, f"project_{step}"
        )
        for at, offset in enumerate(offsets):
            gates[offset] = (rows, at)
        ring[peers - step], ring[step] = below, above
        below, above, state = lax.optimization_barrier((below, above, state))
    att, rows = last_shard(
        sz, place, below, above, w, q_gain.reshape(1, -1), k_gain.reshape(1, -1), state
    )
    gates[far] = (rows, 0)
    early = [far - 1, far, far + 1]
    late = [o for d in range(far - 2, 0, -1) for o in (d, peers - d)] + [0]
    parts = {}
    for name, group in (("parts_far", early), ("parts_near", late)):
        made = output_parts(sz, place, group, [gates[o] for o in group], w_out, coef, att, name)
        for offset, part in zip(group, made):
            parts[offset] = shifted(part, offset) if offset else part
    total = parts[0].astype(jnp.float32)
    for offset in early + late[:-1]:
        total = total + parts[offset].astype(jnp.float32)
    total = total.reshape(images, image_len, width)
    return (image_latents.astype(jnp.float32) * coef_total[:, None, None] + total).astype(jnp.bfloat16)


def solution(mesh):
    placed = (
        P("dp", None, "mp"),
        P("dp", None, "mp"),
        P("dp", None, "mp"),
        P(None, None, "mp"),
        P("mp", None),
        P(),
        P(),
        P("dp"),
        P("dp"),
        P("dp"),
    )
    return jax.shard_map(
        on_device, mesh=mesh, in_specs=placed, out_specs=P("dp", None, "mp"), check_vma=False
    )
```
